32 devices in a mesh: row: 8 (over z, y), col: 4 (over x, core).
Axes of the slice: x: 2, y: 2, z: 4, core: 2. Of those that a mesh axis runs over, the one named last changes fastest.
Arguments:
- entries: int32 [32, 16, 128, 128], P('row', 'col'), may hold values from -2 to 2
- tile_cols: int32 [32, 16], P('row', 'col'), may hold values from 0 to 31
- block_now: int32 [32, 16384], P(None, ('col', 'row')), may hold values from 0 to 65520
- block_prev: int32 [32, 16384], P(None, ('col', 'row')), may hold values from 0 to 65520
- block_prev2: int32 [32, 16384], P(None, ('col', 'row')), may hold values from 0 to 65520
- gram_prev: int32 [32, 32], replicated, may hold values from 0 to 65520
- square_prev: int32 [32, 32], replicated, may hold values from 0 to 65520
- inverse_prev: int32 [32, 32], replicated, may hold values from 0 to 65520
- inverse_prev2: int32 [32, 32], replicated, may hold values from 0 to 65520
Outputs:
- next_block: float32 [32, 16384], P(None, ('col', 'row'))
- later_block: float32 [32, 16384], P(None, ('col', 'row'))
The draws below stay inside these ranges and needn't reach their ends.
Inputs may be any that keep to these rules, and one draw needn't show every extreme that they name: `tile_cols`: stored tiles that name the same tile column in one tile row add. `block_prev`: residues. `block_prev2`: residues. `gram_prev`: residues. `square_prev`: residues. `inverse_prev`: residues. `inverse_prev2`: residues.
All inputs are finite; a program needn't handle non-finite values.
Results may differ from the reference program's by a relative error of at most 0.0003.
Values sent between devices are 32-bit elements; how exact they have to be, the bound alone decides.
A program may use at most 64 MiB of HBM per device.

```python
import jax
import jax.numpy as jnp
from jax import lax

BLOCK = 32
TILE = 128
SLOTS = 4
TCOLS = 32
ORDER = 16384
TROWS_ALL = 32
SLOTS_ALL = 16
N_COL = 4


def with_ends(values, key, least, top_value):
    extent = values.shape
    index_at = [jax.random.randint(jax.random.fold_in(key, axis), (), 0, extent[axis]) for axis in range(len(extent))]
    values = values.at[tuple(index_at)].set(least)
    longest = extent.index(max(extent))
    index_at[longest] = (index_at[longest] + 1) % extent[longest]
    return values.at[tuple(index_at)].set(top_value)


def setup_inputs(seed: int = 0) -> dict:
    seeds = jax.random.split(jax.random.key(seed), 10)
    return {
        "entries": with_ends(jax.random.randint(seeds[0], (TROWS_ALL, SLOTS_ALL, TILE, TILE), -2, 3), jax.random.fold_in(seeds[0], 1), -2, 2).astype(jnp.int32),
        "tile_cols": with_ends(jax.random.randint(seeds[1], (TROWS_ALL, SLOTS_ALL), 0, TCOLS), jax.random.fold_in(seeds[1], 1), 0, TCOLS - 1).astype(jnp.int32),
        "block_now": with_ends(jax.random.randint(seeds[2], (BLOCK, ORDER), 0, 65521), jax.random.fold_in(seeds[2], 1), 0, 65520).astype(jnp.int32),
        "block_prev": with_ends(jax.random.randint(seeds[3], (BLOCK, ORDER), 0, 65521), jax.random.fold_in(seeds[3], 1), 0, 65520).astype(jnp.int32),
        "block_prev2": with_ends(jax.random.randint(seeds[4], (BLOCK, ORDER), 0, 65521), jax.random.fold_in(seeds[4], 1), 0, 65520).astype(jnp.int32),
        "gram_prev": with_ends(jax.random.randint(seeds[5], (BLOCK, BLOCK), 0, 65521), jax.random.fold_in(seeds[5], 1), 0, 65520).astype(jnp.int32),
        "square_prev": with_ends(jax.random.randint(seeds[6], (BLOCK, BLOCK), 0, 65521), jax.random.fold_in(seeds[6], 1), 0, 65520).astype(jnp.int32),
        "inverse_prev": with_ends(jax.random.randint(seeds[7], (BLOCK, BLOCK), 0, 65521), jax.random.fold_in(seeds[7], 1), 0, 65520).astype(jnp.int32),
        "inverse_prev2": with_ends(jax.random.randint(seeds[8], (BLOCK, BLOCK), 0, 65521), jax.random.fold_in(seeds[8], 1), 0, 65520).astype(jnp.int32),
    }


modulus = 65521.0


def residue(values):
    return jnp.mod(values, modulus)


def split_digits(values):
    top_part = jnp.floor(values / 256.0)
    return top_part, values - top_part * 256.0


def fold_digits(top_sum, low_sum):
    return residue(residue(residue(top_sum) * 256.0) + residue(low_sum))


def fold_three(upper_part, middle, lower_part):
    return residue(residue(residue(upper_part) * 15.0) + residue(residue(middle) * 256.0) + residue(lower_part))


def mulmod(left_side, right_side):
    top_part, low_part = split_digits(right_side)
    return fold_digits(left_side * top_part, left_side * low_part)


def exact_dot(left_side, right_side):
    return jnp.dot(left_side, right_side, precision=lax.Precision.HIGHEST, preferred_element_type=jnp.float32)


def small_product(left_side, right_side):
    left_top, left_low = split_digits(left_side)
    right_top, right_low = split_digits(right_side)
    return fold_three(exact_dot(left_top, right_top), exact_dot(left_top, right_low) + exact_dot(left_low, right_top), exact_dot(left_low, right_low))


def inverse_scalar(number):
    result = jnp.ones_like(number)
    square = number
    exponent = 65519
    for position in range(16):
        if (exponent >> position) & 1:
            result = mulmod(result, square)
        square = mulmod(square, square)
    return result


def inverse_matrix(matrix):
    matrix_order = matrix.shape[0]
    augmented = jnp.concatenate([matrix, jnp.eye(matrix_order, dtype=matrix.dtype)], axis=1)
    row_numbers = jnp.arange(matrix_order, dtype=jnp.int32)

    def eliminate(column, augmented):
        column = jnp.asarray(column).astype(jnp.int32)
        pivot_column = augmented[:, column]
        usable = (pivot_column != 0.0) & (row_numbers >= column)
        pivot_row_id = jnp.where(jnp.any(usable), jnp.argmax(usable).astype(jnp.int32), column)
        pivot_row = augmented[pivot_row_id]
        current_row = augmented[column]
        swapped = jnp.where((row_numbers == column)[:, None], pivot_row[None, :], jnp.where((row_numbers == pivot_row_id)[:, None], current_row[None, :], augmented))
        scaled = mulmod(pivot_row, inverse_scalar(pivot_row[column]))
        factors = jnp.where(row_numbers == column, 0.0, swapped[:, column])
        reduced = residue(swapped - mulmod(factors[:, None], scaled[None, :]) + modulus)
        return jnp.where((row_numbers == column)[:, None], scaled[None, :], reduced)

    augmented = lax.fori_loop(0, matrix_order, eliminate, augmented)
    return augmented[:, matrix_order:]


def coefficients(gram_now, square_now, inverse_now, inverse_prev, inverse_prev2, gram_old, square_old):
    identity = jnp.eye(gram_now.shape[0], dtype=gram_now.dtype)
    first = residue(identity - small_product(residue(square_now + gram_now), inverse_now) + modulus)
    second = residue(modulus - small_product(gram_now, inverse_prev))
    middle = residue(identity - small_product(inverse_prev, gram_old) + modulus)
    third = residue(modulus - small_product(small_product(residue(square_old + gram_old), middle), inverse_prev2))
    return jnp.concatenate([first, second, third], axis=1)


def combine_blocks(coeffs, stacked):
    coeff_top, coeff_low = split_digits(coeffs)
    stack_top, stack_low = split_digits(stacked)
    left_side = jnp.stack([coeff_top, coeff_low])
    right_side = jnp.stack([stack_top, stack_low])
    products = jnp.einsum('dab,ebn->dean', left_side, right_side, precision=lax.Precision.HIGHEST)
    return fold_three(products[0, 0], products[0, 1] + products[1, 0], products[1, 1])


def gram_whole(first, second):
    column_count = first.shape[1]
    group_width = min(column_count, 128)
    groups = column_count // group_width
    first_digits = jnp.stack(split_digits(first)).reshape(2, first.shape[0], groups, group_width)
    second_digits = jnp.stack(split_digits(second)).reshape(2, second.shape[0], groups, group_width)
    products = jnp.einsum('dagw,ecgw->gdeac', first_digits, second_digits, precision=lax.Precision.HIGHEST)
    per_group = fold_three(products[:, 0, 0], products[:, 0, 1] + products[:, 1, 0], products[:, 1, 1])
    top_part, low_part = split_digits(per_group)
    return fold_digits(jnp.sum(top_part, axis=0), jnp.sum(low_part, axis=0))


def reference(entries, tile_cols, block_now, block_prev, block_prev2, gram_prev, square_prev, inverse_prev, inverse_prev2):
    col_tiles = TCOLS * N_COL
    slot_owner = (jnp.arange(SLOTS * N_COL, dtype=jnp.int32) // SLOTS) * TCOLS
    global_cols = (tile_cols + slot_owner[None, :]).astype(jnp.int32)

    def apply_operator(block):
        top_part, low_part = split_digits(block)
        digits = jnp.concatenate([top_part, low_part], axis=0).reshape(2 * BLOCK, col_tiles, TILE)

        def per_row(running, inputs):
            tile_row, cols_row = inputs
            matrix = tile_row.astype(jnp.float32)
            picked = jnp.take(digits, cols_row, axis=1)
            raw_sums = jnp.einsum('bsk,sjk->bj', picked, matrix, precision=lax.Precision.HIGHEST)
            projected = fold_digits(raw_sums[:BLOCK], raw_sums[BLOCK:])
            proj_top, proj_low = split_digits(projected)
            proj_digits = jnp.concatenate([proj_top, proj_low], axis=0)
            spread = jnp.einsum('bj,sjk->bsk', proj_digits, matrix, precision=lax.Precision.HIGHEST)
            per_slot = fold_digits(spread[:BLOCK], spread[BLOCK:])
            return residue(running.at[:, cols_row, :].add(per_slot)), None

        totals, unused = lax.scan(per_row, jnp.zeros((BLOCK, col_tiles, TILE), jnp.float32), (entries, global_cols))
        return totals.reshape(BLOCK, col_tiles * TILE)

    current = block_now.astype(jnp.float32)
    earlier = block_prev.astype(jnp.float32)
    earliest = block_prev2.astype(jnp.float32)
    gram_old = gram_prev.astype(jnp.float32)
    square_old = square_prev.astype(jnp.float32)
    inverse_old = inverse_prev.astype(jnp.float32)
    inverse_older = inverse_prev2.astype(jnp.float32)
    results = []
    for iteration in range(2):
        applied = apply_operator(current)
        gram_now = gram_whole(current, applied)
        square_now = gram_whole(applied, applied)
        inverse_now = inverse_matrix(gram_now)
        coeffs = coefficients(gram_now, square_now, inverse_now, inverse_old, inverse_older, gram_old, square_old)
        stacked = jnp.concatenate([current, earlier, earliest], axis=0)
        following = residue(applied + combine_blocks(coeffs, stacked))
        results.append(following / modulus)
        earliest, earlier, current = earlier, current, following
        inverse_older, inverse_old = inverse_old, inverse_now
        gram_old, square_old = gram_now, square_now
    return results[0], results[1]
```

```python
import functools

import jax
import jax.numpy as jnp
from jax import lax
from jax.experimental import pallas as pl
from jax.experimental.pallas import tpu as pltpu
from jax.sharding import PartitionSpec as P

modulus = 65521.0
reciprocal = 1.0 / 65521.0
MESH = pl.DeviceIdType.MESH
BLOCKS_OUT, PARTIAL_OUT, GRAM_OUT, SQUARE_ROW_OUT, SQUARE_COL_OUT, SQUARE_ALL_OUT = 0, 2, 4, 5, 6, 7
PARTIAL_IN, GRAM_IN, SQUARE_ROW_IN, SQUARE_COL_IN, SQUARE_ALL_IN = 0, 2, 3, 4, 5


def near(values):
    return values - jnp.floor(values * reciprocal + 0.5) * modulus


def whole(values):
    signed = near(values)
    return jnp.where(signed < 0.0, signed + modulus, signed)


def split(values):
    top = jnp.floor(values * (1.0 / 256.0) + 0.5)
    return top, values - top * 256.0


def digits(values):
    top, low = split(values)
    return jnp.concatenate([top, low], axis=0).astype(jnp.bfloat16)


def fold_two(top, low):
    return near(near(top) * 256.0 + low)


def fold_three(upper, middle, lower):
    return near(near(upper) * 15.0 + near(middle) * 256.0 + near(lower))


def mulmod(left, right):
    top, low = split(right)
    return near(near(left * top) * 256.0 + left * low)


def dot(left, right):
    return jnp.dot(left, right, preferred_element_type=jnp.float32)


def dot_t(left, right):
    return lax.dot_general(
        left, right, (((1,), (1,)), ((), ())), preferred_element_type=jnp.float32
    )


def product_parts(left, right):
    order = left.shape[0]
    left_digits = digits(left)
    right_top, right_low = split(right)
    with_top = dot(left_digits, right_top.astype(jnp.bfloat16))
    with_low = dot(left_digits, right_low.astype(jnp.bfloat16))
    return with_top[:order], with_top[order:] + with_low[:order], with_low[order:]


def small_product(left, right):
    return fold_three(*product_parts(left, right))


def gram_tiles(tiles):
    order = tiles[0].shape[0]
    total = None
    for tile in tiles:
        both = digits(tile)
        term = dot_t(both, both)
        total = term if total is None else total + term
    return fold_three(
        total[:order, :order],
        total[:order, order:] + total[order:, :order],
        total[order:, order:],
    )


def power_inverse(number):
    result = None
    square = number
    for position in range(16):
        if 65519 >> position & 1:
            result = square if result is None else mulmod(result, square)
        if position < 15:
            square = mulmod(square, square)
    return result


def identity_of(order):
    rows = lax.broadcasted_iota(jnp.int32, (order, order), 0)
    lanes = lax.broadcasted_iota(jnp.int32, (order, order), 1)
    return jnp.where(rows == lanes, 1.0, 0.0).astype(jnp.float32)


class Elimination:
    def __init__(self, matrix):
        self.order = matrix.shape[0]
        self.done = 0
        self.work = jnp.concatenate([matrix, identity_of(self.order)], axis=1)

    def advance(self, columns):
        last = min(self.order, self.done + columns)
        for column in range(self.done, last):
            self.work = eliminated(self.work, column)
        self.done = last

    def result(self):
        self.advance(self.order)
        left = self.work[:, : self.order]
        diagonal = jnp.sum(left * identity_of(self.order), axis=1, keepdims=True)
        return mulmod(self.work[:, self.order :], power_inverse(diagonal))


def eliminated(work, column):
    order = work.shape[0]
    rows = lax.broadcasted_iota(jnp.int32, (order, 1), 0)
    entry = work[:, column : column + 1]
    usable = (entry != 0.0) & (rows >= column)
    first = jnp.min(jnp.where(usable, rows, order), axis=0, keepdims=True)
    chosen = rows == jnp.where(first == order, column, first)
    pivot_row = jnp.sum(jnp.where(chosen, work, 0.0), axis=0, keepdims=True)
    pivot = jnp.sum(jnp.where(chosen, entry, 0.0), axis=0, keepdims=True)
    swapped = jnp.where(chosen, work[column : column + 1, :], work)
    factor = jnp.where(chosen, entry[column : column + 1, :], entry)
    pivot_row = jnp.where(pivot == 0.0, 0.0, pivot_row)
    pivot = jnp.where(pivot == 0.0, 1.0, pivot)
    pivot_top, pivot_low = split(pivot)
    factor_top, factor_low = split(factor)
    upper = near(pivot_top * swapped - factor_top * pivot_row)
    reduced = near(upper * 256.0 + (pivot_low * swapped - factor_low * pivot_row))
    return jnp.where(rows == column, pivot_row, reduced)


def pack(values):
    rows = values.shape[0] // 4
    return jnp.concatenate([values[g * rows : (g + 1) * rows] for g in range(4)], axis=1)


def unpack(values):
    width = values.shape[1] // 4
    return jnp.concatenate([values[:, g * width : (g + 1) * width] for g in range(4)], axis=0)


def direct_squares(n_row, n_col):
    return n_row * n_col <= 64


def flipped(place, mask, count):
    assert count & (count - 1) == 0
    bit = 1
    moved = place
    while bit < count:
        if mask & bit:
            moved = moved + bit - 2 * bit * lax.rem(place // bit, 2)
        bit *= 2
    return moved


def kernel(
    n_row, n_col, cols_ref,
    entries_hbm, now_hbm, prev_hbm, prev2_hbm,
    gram_hbm, square_hbm, inverse_hbm, inverse2_hbm, next_hbm, later_hbm,
    entries_ref, now_ref, older_ref, small_ref, next_ref, later_ref,
    tile16, full_a, full_b, partial, spread, running, outgoing, incoming,
    gram_buf, square_row, square_col, square_all, order_ref, begin_ref,
    local_sem, send_sem, recv_sem, block_sem,
):
    my_row = lax.axis_index("row")
    my_col = lax.axis_index("col")
    tile_rows, slots, size = entries_ref.shape[:3]
    stored = tile_rows * slots
    order = now_ref.shape[0]
    share = now_ref.shape[1] // size
    half = n_row // 2
    direct = direct_squares(n_row, n_col)

    def row_peer(m):
        return flipped(my_row, m, n_row)

    def col_peer(m):
        return flipped(my_col, m, n_col)

    arrivals = [(now_hbm, now_ref, 0), (entries_hbm, entries_ref, 1)]
    arrivals += [(prev_hbm, older_ref.at[0], 2), (prev2_hbm, older_ref.at[1], 2)]
    for i, source in enumerate([gram_hbm, square_hbm, inverse_hbm, inverse2_hbm]):
        arrivals.append((source, small_ref.at[i], 3))
    copies_in = [
        pltpu.make_async_copy(source, target, local_sem.at[i]) for source, target, i in arrivals
    ]

    def local_wait(ref, i):
        pltpu.make_async_copy(ref, ref, local_sem.at[i]).wait()

    pairs = [(m, k) for k in range(n_col) for m in range(n_row) if m or k]
    if not direct:
        pairs = [(m, k) for m, k in pairs if m == 0 or k == 0]
    copies_in[0].start()
    barrier = pltpu.get_barrier_semaphore()
    for m, k in pairs:
        pl.semaphore_signal(
            barrier, inc=1, device_id=(row_peer(m), col_peer(k)), device_id_type=MESH
        )
    for copy in copies_in[1:]:
        copy.start()

    def remote(source, target, out, into, device):
        return pltpu.make_async_remote_copy(
            src_ref=source, dst_ref=target, send_sem=out, recv_sem=into,
            device_id=device, device_id_type=MESH,
        )

    def send(source, target, out, into, device):
        copy = remote(source, target, send_sem.at[out], into, device)
        copy.start()
        return copy

    def wait_in(ref, into):
        remote(ref, ref, send_sem.at[0], into, (my_row, my_col)).wait_recv()

    def wait_out(ref, out):
        remote(ref, ref, send_sem.at[out], recv_sem.at[0], (my_row, my_col)).wait_send()

    def tiles_of(values):
        return [values[:, t * size : (t + 1) * size] for t in range(share)]

    def load(ref):
        return tiles_of(near(ref[...].astype(jnp.float32)))

    def block(full, row):
        return full.at[pl.ds(row * share, share)]

    local_wait(now_ref, 0)
    current = load(now_ref)
    for t in range(share):
        full_a[my_row * share + t] = current[t]
    pl.semaphore_wait(barrier, len(pairs))

    def gather_start(step, full):
        mine = block(full, my_row)
        for m in range(1, half):
            send(mine, mine, BLOCKS_OUT + step, block_sem.at[m], (row_peer(2 * m), my_col))
        send(mine, mine, BLOCKS_OUT + step, block_sem.at[0], (row_peer(1), my_col))

    def gather_pass(step, full, m):
        got = block(full, row_peer(2 * m))
        wait_in(got, block_sem.at[m])
        send(got, got, BLOCKS_OUT + step, block_sem.at[0], (row_peer(1), my_col))

    def gather_end(full):
        wait_in(full.at[pl.ds(0, half * share)], block_sem.at[0])

    def third_of():
        middle = near(identity - small_product(inverse_old, gram_old))
        return -small_product(
            small_product(near(square_old + gram_old), middle), inverse_older
        )

    gather_start(0, full_a)
    local_wait(entries_ref, 1)
    for i in range(stored):
        tile16[i] = entries_ref[i // slots, i % slots].astype(jnp.float32).astype(jnp.bfloat16)
    local_wait(older_ref, 2)
    local_wait(small_ref, 3)
    earlier, earliest = load(older_ref.at[0]), load(older_ref.at[1])
    gram_old = near(small_ref[0].astype(jnp.float32))
    square_old = near(small_ref[1].astype(jnp.float32))
    inverse_old = near(small_ref[2].astype(jnp.float32))
    inverse_older = near(small_ref[3].astype(jnp.float32))
    identity = identity_of(order)
    cols = [cols_ref[i // slots, i % slots] for i in range(stored)]

    def as_int(flag):
        return jnp.where(flag, 1, 0).astype(jnp.int32)

    third = third_of()

    for m in range(1, half):
        gather_pass(0, full_a, m)
        if m == 1:
            ranks = []
            for i in range(stored):
                rank = jnp.int32(0)
                for j in range(stored):
                    if j != i:
                        rank = rank + as_int(
                            cols[j] <= cols[i] if j < i else cols[j] < cols[i]
                        )
                ranks.append(rank)
            for k in range(stored):
                place = jnp.int32(0)
                for i in range(1, stored):
                    place = place + jnp.where(ranks[i] == k, i, 0).astype(jnp.int32)
                order_ref[k] = place

    def count(tile, carry):
        below = jnp.int32(0)
        for i in range(stored):
            below = below + as_int(cols[i] < tile)
        begin_ref[tile] = below
        return carry

    lax.fori_loop(0, n_row * share + 1, count, 0)
    gather_end(full_a)

    def forward(step, full):
        for r in range(tile_rows):
            total = None
            for s in range(slots):
                picked = full[cols[r * slots + s]]
                term = dot_t(digits(picked), tile16[r * slots + s])
                total = term if total is None else total + term
            partial[step, my_col, r] = fold_two(total[:order], total[order:])
            own = partial.at[step, my_col, r]
            for m in range(1, n_col):
                send(
                    own, own, PARTIAL_OUT + step, recv_sem.at[PARTIAL_IN + step],
                    (my_row, col_peer(m)),
                )

    def partial_end(step):
        wait_in(partial.at[step, pl.ds(0, n_col - 1)], recv_sem.at[PARTIAL_IN + step])

    def summed_partial(step, r):
        total = partial[step, 0, r]
        for c in range(1, n_col):
            total = total + partial[step, c, r]
        return total

    forward(0, full_a)
    partial_end(0)
    projected = [near(summed_partial(0, r)) for r in range(tile_rows)]

    def summed(buffer, count):
        total = buffer[0]
        for r in range(1, count):
            total = total + buffer[r]
        return near(total)

    def to_row(buffer, out, into):
        own = buffer.at[my_row]
        for m in range(1, n_row):
            send(own, own, out, recv_sem.at[into], (row_peer(m), my_col))

    def from_row(buffer, out, into):
        others = buffer.at[pl.ds(0, n_row - 1)]
        wait_in(others, recv_sem.at[into])
        wait_out(others, out)
        return summed(buffer, n_row)

    def square_rows(applied):
        square_row[my_row] = pack(gram_tiles(applied))
        to_row(square_row, SQUARE_ROW_OUT, SQUARE_ROW_IN)

    def square_cols():
        square_col[my_col] = from_row(square_row, SQUARE_ROW_OUT, SQUARE_ROW_IN)
        own = square_col.at[my_col]
        for m in range(1, n_col):
            send(own, own, SQUARE_COL_OUT, recv_sem.at[SQUARE_COL_IN], (my_row, col_peer(m)))

    def square_end():
        others = square_col.at[pl.ds(0, n_col - 1)]
        wait_in(others, recv_sem.at[SQUARE_COL_IN])
        wait_out(others, SQUARE_COL_OUT)
        return unpack(summed(square_col, n_col))

    def square_direct(applied):
        mine = my_row * n_col + my_col
        square_all[mine] = pack(gram_tiles(applied))
        own = square_all.at[mine]
        for m, k in reversed(pairs):
            send(
                own, own, SQUARE_ALL_OUT, recv_sem.at[SQUARE_ALL_IN],
                (row_peer(m), col_peer(k)),
            )

    for step in range(2):
        gram_buf[step, my_row] = pack(gram_tiles(projected))
        to_row(gram_buf.at[step], GRAM_OUT, GRAM_IN)

        for r in range(tile_rows):
            both = digits(projected[r])
            for s in range(slots):
                spread[r * slots + s] = dot(both, tile16[r * slots + s])
        total = jnp.zeros((2 * order, size), jnp.float32)
        running[0] = total
        for i in range(stored):
            total = total + spread[order_ref[i]]
            running[i + 1] = total

        def finish_block(peer):
            for t in range(share):
                tile = peer * share + t
                sums = running[begin_ref[tile + 1]] - running[begin_ref[tile]]
                outgoing[step, tile] = fold_two(sums[:order], sums[order:])

        for m in range(half - 1, -1, -1):
            peer = row_peer(2 * m + 1)
            finish_block(peer)
            send(
                block(outgoing.at[step], peer), incoming.at[step, m], BLOCKS_OUT + step,
                block_sem.at[half + m], (row_peer(1), my_col),
            )
        for m in range(half - 1, -1, -1):
            finish_block(row_peer(2 * m))
        if step:
            third = third_of()
        for m in range(half - 1, 0, -1):
            wait_in(incoming.at[step, m], block_sem.at[half + m])
            peer = row_peer(2 * m)
            for t in range(share):
                outgoing[step, peer * share + t] = (
                    outgoing[step, peer * share + t] + incoming[step, m, t]
                )
            send(
                block(outgoing.at[step], peer), incoming.at[step, half + m], BLOCKS_OUT + step,
                block_sem.at[half], (peer, my_col),
            )

        gram_now = unpack(from_row(gram_buf.at[step], GRAM_OUT, GRAM_IN))
        inverting = Elimination(gram_now)
        second = -small_product(gram_now, inverse_old)
        parts = []
        for t in range(share):
            one = product_parts(second, earlier[t])
            two = product_parts(third, earliest[t])
            upper, mid, lower = [a + b for a, b in zip(one, two)]
            parts.append(near(upper) * 15.0 + near(mid) * 256.0 + lower)
        if step:
            inverting.advance(16)

        wait_in(incoming.at[step, pl.ds(0, half)], block_sem.at[half])
        applied = []
        for t in range(share):
            total = outgoing[step, my_row * share + t]
            for m in [0] + list(range(half + 1, n_row)):
                total = total + incoming[step, m, t]
            applied.append(near(total))

        if step == 0:
            ready = [near(applied[t] + parts[t]) for t in range(share)]
            for t in range(share):
                full_b[my_row * share + t] = ready[t]
            gather_start(1, full_b)
            square_rows(applied)
            inverting.advance(14)
            for m in range(1, half):
                gather_pass(1, full_b, m)
                inverting.advance(6)
            inverse_now = inverting.result()
            square_cols()
            gather_end(full_b)
            forward(1, full_b)
            square_now = square_end()
            first = near(
                identity - small_product(near(square_now + gram_now), inverse_now)
            )
            rest = [fold_three(*product_parts(first, projected[r])) for r in range(tile_rows)]
            following = []
            for t in range(share):
                upper, mid, lower = product_parts(first, current[t])
                following.append(
                    whole(ready[t] + near(upper) * 15.0 + near(mid) * 256.0 + lower)
                )
                next_ref[:, t * size : (t + 1) * size] = following[t]
            next_out = pltpu.make_async_copy(next_ref, next_hbm, local_sem.at[0])
            next_out.start()
            partial_end(1)
            projected = [near(summed_partial(1, r) + rest[r]) for r in range(tile_rows)]
            earliest, earlier, current = earlier, current, [near(f) for f in following]
            inverse_older, inverse_old = inverse_old, inverse_now
            gram_old, square_old = gram_now, square_now
            continue

        if direct:
            square_direct(applied)
        else:
            square_rows(applied)
        inverse_now = inverting.result()
        turned = [small_product(inverse_now, current[t]) for t in range(share)]
        before = []
        for t in range(share):
            upper, mid, lower = product_parts(gram_now, turned[t])
            done = near(upper) * 15.0 + near(mid) * 256.0 + lower
            before.append(near(near(applied[t] + parts[t]) + current[t] - done))
        if direct:
            others = square_all.at[pl.ds(0, n_row * n_col - 1)]
            wait_in(others, recv_sem.at[SQUARE_ALL_IN])
            wait_out(others, SQUARE_ALL_OUT)
            square_now = unpack(summed(square_all, n_row * n_col))
        else:
            square_cols()
            square_now = square_end()
        for t in range(share):
            upper, mid, lower = product_parts(square_now, turned[t])
            done = near(upper) * 15.0 + near(mid) * 256.0 + lower
            later_ref[:, t * size : (t + 1) * size] = whole(before[t] - done)
        later_out = pltpu.make_async_copy(later_ref, later_hbm, local_sem.at[1])
        later_out.start()

    for step in range(2):
        wait_out(outgoing.at[:, pl.ds(0, (n_row - 1) * share)], BLOCKS_OUT + step)
        wait_out(partial.at[step, pl.ds(0, n_col - 1)], PARTIAL_OUT + step)
    next_out.wait()
    later_out.wait()


def body(
    n_row, n_col, entries, tile_cols, block_now, block_prev, block_prev2,
    gram_prev, square_prev, inverse_prev, inverse_prev2,
):
    tile_rows, slots, size = entries.shape[:3]
    order, width = block_now.shape
    share = width // size
    col_tiles = n_row * share
    stored = tile_rows * slots
    assert tile_rows <= 4 and share <= 4 and n_row % 2 == 0

    f32 = jnp.float32
    smem = pl.BlockSpec(memory_space=pltpu.SMEM)
    anywhere = pl.BlockSpec(memory_space=pl.ANY)
    devices = n_row * n_col if direct_squares(n_row, n_col) else 1
    packed = (order // 4, order * 4)
    following, later = pl.pallas_call(
        functools.partial(kernel, n_row, n_col),
        out_shape=(jax.ShapeDtypeStruct((order, width), f32),) * 2,
        in_specs=[smem] + [anywhere] * 8,
        out_specs=(anywhere, anywhere),
        scratch_shapes=[
            pltpu.VMEM(entries.shape, jnp.int32),
            pltpu.VMEM((order, width), jnp.int32),
            pltpu.VMEM((2, order, width), jnp.int32),
            pltpu.VMEM((4, order, order), jnp.int32),
            *[pltpu.VMEM((order, width), f32)] * 2,
            pltpu.VMEM((stored, size, size), jnp.bfloat16),
            pltpu.VMEM((col_tiles, order, size), f32),
            pltpu.VMEM((col_tiles, order, size), f32),
            pltpu.VMEM((2, n_col, tile_rows, order, size), f32),
            pltpu.VMEM((stored, 2 * order, size), f32),
            pltpu.VMEM((stored + 1, 2 * order, size), f32),
            pltpu.VMEM((2, col_tiles, order, size), f32),
            pltpu.VMEM((2, n_row, share, order, size), f32),
            pltpu.VMEM((2, n_row) + packed, f32),
            pltpu.VMEM((n_row,) + packed, f32),
            pltpu.VMEM((n_col,) + packed, f32),
            pltpu.VMEM((devices,) + packed, f32),
            pltpu.SMEM((stored,), jnp.int32),
            pltpu.SMEM((col_tiles + 1,), jnp.int32),
            pltpu.SemaphoreType.DMA((4,)),
            pltpu.SemaphoreType.DMA((8,)),
            pltpu.SemaphoreType.DMA((6,)),
            pltpu.SemaphoreType.DMA((n_row,)),
        ],
        compiler_params=pltpu.CompilerParams(collective_id=0, has_side_effects=True),
    )(
        tile_cols, entries, block_now, block_prev, block_prev2,
        gram_prev, square_prev, inverse_prev, inverse_prev2,
    )
    return following / modulus, later / modulus


def solution(mesh):
    placed = (
        P("row", "col", None, None),
        P("row", "col"),
        P(None, ("col", "row")),
        P(None, ("col", "row")),
        P(None, ("col", "row")),
        P(),
        P(),
        P(),
        P(),
    )
    return jax.shard_map(
        functools.partial(body, mesh.shape["row"], mesh.shape["col"]),
        mesh=mesh,
        in_specs=placed,
        out_specs=(P(None, ("col", "row")), P(None, ("col", "row"))),
        check_vma=False,
    )
```

```python
import functools

import jax
import jax.numpy as jnp
from jax import lax
from jax.experimental import pallas as pl
from jax.experimental.pallas import tpu as pltpu
from jax.sharding import PartitionSpec as P

modulus = 65521.0
reciprocal = 1.0 / 65521.0
MESH = pl.DeviceIdType.MESH
BLOCKS_OUT, PARTIAL_OUT, GRAM_OUT, SQUARE_ROW_OUT, SQUARE_COL_OUT, SQUARE_ALL_OUT = 0, 2, 4, 5, 6, 7
PARTIAL_IN, GRAM_IN, SQUARE_ROW_IN, SQUARE_COL_IN, SQUARE_ALL_IN = 0, 2, 3, 4, 5


def near(values):
    return values - jnp.floor(values * reciprocal + 0.5) * modulus


def whole(values):
    signed = near(values)
    return jnp.where(signed < 0.0, signed + modulus, signed)


def split(values):
    top = jnp.floor(values * (1.0 / 256.0) + 0.5)
    return top, values - top * 256.0


def digits(values):
    top, low = split(values)
    return jnp.concatenate([top, low], axis=0).astype(jnp.bfloat16)


def fold_two(top, low):
    return near(near(top) * 256.0 + low)


def fold_three(upper, middle, lower):
    return near(near(upper) * 15.0 + near(middle) * 256.0 + near(lower))


def mulmod(left, right):
    top, low = split(right)
    return near(near(left * top) * 256.0 + left * low)


def dot(left, right):
    return jnp.dot(left, right, preferred_element_type=jnp.float32)


def dot_t(left, right):
    return lax.dot_general(
        left, right, (((1,), (1,)), ((), ())), preferred_element_type=jnp.float32
    )


def product_parts(left, right):
    order = left.shape[0]
    left_digits = digits(left)
    right_top, right_low = split(right)
    with_top = dot(left_digits, right_top.astype(jnp.bfloat16))
    with_low = dot(left_digits, right_low.astype(jnp.bfloat16))
    return with_top[:order], with_top[order:] + with_low[:order], with_low[order:]


def small_product(left, right):
    return fold_three(*product_parts(left, right))


def gram_tiles(tiles):
    order = tiles[0].shape[0]
    total = None
    for tile in tiles:
        both = digits(tile)
        term = dot_t(both, both)
        total = term if total is None else total + term
    return fold_three(
        total[:order, :order],
        total[:order, order:] + total[order:, :order],
        total[order:, order:],
    )


def power_inverse(number):
    result = None
    square = number
    for position in range(16):
        if 65519 >> position & 1:
            result = square if result is None else mulmod(result, square)
        if position < 15:
            square = mulmod(square, square)
    return result


def identity_of(order):
    rows = lax.broadcasted_iota(jnp.int32, (order, order), 0)
    lanes = lax.broadcasted_iota(jnp.int32, (order, order), 1)
    return jnp.where(rows == lanes, 1.0, 0.0).astype(jnp.float32)


class Elimination:
    def __init__(self, matrix):
        self.order = matrix.shape[0]
        self.done = 0
        self.work = jnp.concatenate([matrix, identity_of(self.order)], axis=1)

    def advance(self, columns):
        last = min(self.order, self.done + columns)
        for column in range(self.done, last):
            self.work = eliminated(self.work, column)
        self.done = last

    def result(self):
        self.advance(self.order)
        left = self.work[:, : self.order]
        diagonal = jnp.sum(left * identity_of(self.order), axis=1, keepdims=True)
        return mulmod(self.work[:, self.order :], power_inverse(diagonal))


def eliminated(work, column):
    order = work.shape[0]
    rows = lax.broadcasted_iota(jnp.int32, (order, 1), 0)
    entry = work[:, column : column + 1]
    usable = (entry != 0.0) & (rows >= column)
    first = jnp.min(jnp.where(usable, rows, order), axis=0, keepdims=True)
    chosen = rows == jnp.where(first == order, column, first)
    pivot_row = jnp.sum(jnp.where(chosen, work, 0.0), axis=0, keepdims=True)
    pivot = jnp.sum(jnp.where(chosen, entry, 0.0), axis=0, keepdims=True)
    swapped = jnp.where(chosen, work[column : column + 1, :], work)
    factor = jnp.where(chosen, entry[column : column + 1, :], entry)
    pivot_row = jnp.where(pivot == 0.0, 0.0, pivot_row)
    pivot = jnp.where(pivot == 0.0, 1.0, pivot)
    pivot_top, pivot_low = split(pivot)
    factor_top, factor_low = split(factor)
    upper = near(pivot_top * swapped - factor_top * pivot_row)
    reduced = near(upper * 256.0 + (pivot_low * swapped - factor_low * pivot_row))
    return jnp.where(rows == column, pivot_row, reduced)


def pack(values):
    rows = values.shape[0] // 4
    return jnp.concatenate([values[g * rows : (g + 1) * rows] for g in range(4)], axis=1)


def unpack(values):
    width = values.shape[1] // 4
    return jnp.concatenate([values[:, g * width : (g + 1) * width] for g in range(4)], axis=0)


def direct_squares(n_row, n_col):
    return n_row * n_col <= 64


def flipped(place, mask, count):
    assert count & (count - 1) == 0
    bit = 1
    moved = place
    while bit < count:
        if mask & bit:
            moved = moved + bit - 2 * bit * lax.rem(place // bit, 2)
        bit *= 2
    return moved


def kernel(
    n_row, n_col, cols_ref,
    entries_hbm, now_hbm, prev_hbm, prev2_hbm,
    gram_hbm, square_hbm, inverse_hbm, inverse2_hbm, next_hbm, later_hbm,
    entries_ref, now_ref, older_ref, small_ref, next_ref, later_ref,
    tile16, full_a, full_b, partial, spread, running, outgoing, incoming,
    gram_buf, square_row, square_col, square_all, order_ref, begin_ref,
    local_sem, send_sem, recv_sem, block_sem, fence_sem,
):
    my_row = lax.axis_index("row")
    my_col = lax.axis_index("col")
    tile_rows, slots, size = entries_ref.shape[:3]
    stored = tile_rows * slots
    order = now_ref.shape[0]
    share = now_ref.shape[1] // size
    half = n_row // 2
    direct = direct_squares(n_row, n_col)

    def row_peer(m):
        return flipped(my_row, m, n_row)

    def col_peer(m):
        return flipped(my_col, m, n_col)

    arrivals = [(now_hbm, now_ref, 0), (entries_hbm, entries_ref, 1)]
    arrivals += [(prev_hbm, older_ref.at[0], 2), (prev2_hbm, older_ref.at[1], 2)]
    for i, source in enumerate([gram_hbm, square_hbm, inverse_hbm, inverse2_hbm]):
        arrivals.append((source, small_ref.at[i], 3))
    copies_in = [
        pltpu.make_async_copy(source, target, local_sem.at[i]) for source, target, i in arrivals
    ]

    def local_wait(ref, i):
        pltpu.make_async_copy(ref, ref, local_sem.at[i]).wait()

    pairs = [(m, k) for k in range(n_col) for m in range(n_row) if m or k]
    if not direct:
        pairs = [(m, k) for m, k in pairs if m == 0 or k == 0]
    copies_in[0].start()
    barrier = pltpu.get_barrier_semaphore()
    for m, k in pairs:
        pl.semaphore_signal(
            barrier, inc=1, device_id=(row_peer(m), col_peer(k)), device_id_type=MESH
        )
    for copy in copies_in[1:]:
        copy.start()

    def remote(source, target, out, into, device):
        return pltpu.make_async_remote_copy(
            src_ref=source, dst_ref=target, send_sem=out, recv_sem=into,
            device_id=device, device_id_type=MESH,
        )

    def send(source, target, out, into, device):
        copy = remote(source, target, send_sem.at[out], into, device)
        copy.start()
        return copy

    def fence():
        pl.semaphore_signal(fence_sem, 1)
        pl.semaphore_wait(fence_sem, 1)

    def wait_in(ref, into):
        remote(ref, ref, send_sem.at[0], into, (my_row, my_col)).wait_recv()

    def wait_out(ref, out):
        remote(ref, ref, send_sem.at[out], recv_sem.at[0], (my_row, my_col)).wait_send()

    def tiles_of(values):
        return [values[:, t * size : (t + 1) * size] for t in range(share)]

    def load(ref):
        return tiles_of(near(ref[...].astype(jnp.float32)))

    def block(full, row):
        return full.at[pl.ds(row * share, share)]

    local_wait(now_ref, 0)
    current = load(now_ref)
    for t in range(share):
        full_a[my_row * share + t] = current[t]
    pl.semaphore_wait(barrier, len(pairs))

    def gather_start(step, full):
        mine = block(full, my_row)
        for m in range(1, half):
            send(mine, mine, BLOCKS_OUT + step, block_sem.at[m], (row_peer(2 * m), my_col))
        send(mine, mine, BLOCKS_OUT + step, block_sem.at[0], (row_peer(1), my_col))
        fence()

    def gather_pass(step, full, m):
        got = block(full, row_peer(2 * m))
        wait_in(got, block_sem.at[m])
        send(got, got, BLOCKS_OUT + step, block_sem.at[0], (row_peer(1), my_col))
        fence()

    def gather_end(full):
        wait_in(full.at[pl.ds(0, half * share)], block_sem.at[0])

    def third_of():
        middle = near(identity - small_product(inverse_old, gram_old))
        return -small_product(
            small_product(near(square_old + gram_old), middle), inverse_older
        )

    gather_start(0, full_a)
    local_wait(entries_ref, 1)
    for i in range(stored):
        tile16[i] = entries_ref[i // slots, i % slots].astype(jnp.float32).astype(jnp.bfloat16)
    local_wait(older_ref, 2)
    local_wait(small_ref, 3)
    earlier, earliest = load(older_ref.at[0]), load(older_ref.at[1])
    gram_old = near(small_ref[0].astype(jnp.float32))
    square_old = near(small_ref[1].astype(jnp.float32))
    inverse_old = near(small_ref[2].astype(jnp.float32))
    inverse_older = near(small_ref[3].astype(jnp.float32))
    identity = identity_of(order)
    cols = [cols_ref[i // slots, i % slots] for i in range(stored)]

    def as_int(flag):
        return jnp.where(flag, 1, 0).astype(jnp.int32)

    third = third_of()

    for m in range(1, half):
        gather_pass(0, full_a, m)
        if m == 1:
            ranks = []
            for i in range(stored):
                rank = jnp.int32(0)
                for j in range(stored):
                    if j != i:
                        rank = rank + as_int(
                            cols[j] <= cols[i] if j < i else cols[j] < cols[i]
                        )
                ranks.append(rank)
            for k in range(stored):
                place = jnp.int32(0)
                for i in range(1, stored):
                    place = place + jnp.where(ranks[i] == k, i, 0).astype(jnp.int32)
                order_ref[k] = place

    def count(tile, carry):
        below = jnp.int32(0)
        for i in range(stored):
            below = below + as_int(cols[i] < tile)
        begin_ref[tile] = below
        return carry

    lax.fori_loop(0, n_row * share + 1, count, 0)
    gather_end(full_a)

    def forward(step, full):
        for r in range(tile_rows):
            total = None
            for s in range(slots):
                picked = full[cols[r * slots + s]]
                term = dot_t(digits(picked), tile16[r * slots + s])
                total = term if total is None else total + term
            partial[step, my_col, r] = fold_two(total[:order], total[order:])
            own = partial.at[step, my_col, r]
            for m in range(1, n_col):
                send(
                    own, own, PARTIAL_OUT + step, recv_sem.at[PARTIAL_IN + step],
                    (my_row, col_peer(m)),
                )
            fence()

    def partial_end(step):
        wait_in(partial.at[step, pl.ds(0, n_col - 1)], recv_sem.at[PARTIAL_IN + step])

    def summed_partial(step, r):
        total = partial[step, 0, r]
        for c in range(1, n_col):
            total = total + partial[step, c, r]
        return total

    forward(0, full_a)
    partial_end(0)
    projected = [near(summed_partial(0, r)) for r in range(tile_rows)]

    def summed(buffer, count):
        total = buffer[0]
        for r in range(1, count):
            total = total + buffer[r]
        return near(total)

    def to_row(buffer, out, into):
        own = buffer.at[my_row]
        for m in range(1, n_row):
            send(own, own, out, recv_sem.at[into], (row_peer(m), my_col))
        fence()

    def from_row(buffer, out, into):
        others = buffer.at[pl.ds(0, n_row - 1)]
        wait_in(others, recv_sem.at[into])
        wait_out(others, out)
        return summed(buffer, n_row)

    def square_rows(applied):
        square_row[my_row] = pack(gram_tiles(applied))
        to_row(square_row, SQUARE_ROW_OUT, SQUARE_ROW_IN)

    def square_cols():
        square_col[my_col] = from_row(square_row, SQUARE_ROW_OUT, SQUARE_ROW_IN)
        own = square_col.at[my_col]
        for m in range(1, n_col):
            send(own, own, SQUARE_COL_OUT, recv_sem.at[SQUARE_COL_IN], (my_row, col_peer(m)))

    def square_end():
        others = square_col.at[pl.ds(0, n_col - 1)]
        wait_in(others, recv_sem.at[SQUARE_COL_IN])
        wait_out(others, SQUARE_COL_OUT)
        return unpack(summed(square_col, n_col))

    def square_direct(applied):
        mine = my_row * n_col + my_col
        square_all[mine] = pack(gram_tiles(applied))
        own = square_all.at[mine]
        for m, k in reversed(pairs):
            send(
                own, own, SQUARE_ALL_OUT, recv_sem.at[SQUARE_ALL_IN],
                (row_peer(m), col_peer(k)),
            )
        fence()

    for step in range(2):
        gram_buf[step, my_row] = pack(gram_tiles(projected))
        to_row(gram_buf.at[step], GRAM_OUT, GRAM_IN)

        for r in range(tile_rows):
            both = digits(projected[r])
            for s in range(slots):
                spread[r * slots + s] = dot(both, tile16[r * slots + s])
        total = jnp.zeros((2 * order, size), jnp.float32)
        running[0] = total
        for i in range(stored):
            total = total + spread[order_ref[i]]
            running[i + 1] = total

        def finish_block(peer):
            for t in range(share):
                tile = peer * share + t
                sums = running[begin_ref[tile + 1]] - running[begin_ref[tile]]
                outgoing[step, tile] = fold_two(sums[:order], sums[order:])

        for m in range(half - 1, -1, -1):
            peer = row_peer(2 * m + 1)
            finish_block(peer)
            send(
                block(outgoing.at[step], peer), incoming.at[step, m], BLOCKS_OUT + step,
                block_sem.at[half + m], (row_peer(1), my_col),
            )
            fence()
        for m in range(half - 1, -1, -1):
            finish_block(row_peer(2 * m))
        if step:
            third = third_of()
        for m in range(half - 1, 0, -1):
            wait_in(incoming.at[step, m], block_sem.at[half + m])
            peer = row_peer(2 * m)
            for t in range(share):
                outgoing[step, peer * share + t] = (
                    outgoing[step, peer * share + t] + incoming[step, m, t]
                )
            send(
                block(outgoing.at[step], peer), incoming.at[step, half + m], BLOCKS_OUT + step,
                block_sem.at[half], (peer, my_col),
            )

        gram_now = unpack(from_row(gram_buf.at[step], GRAM_OUT, GRAM_IN))
        inverting = Elimination(gram_now)
        second = -small_product(gram_now, inverse_old)
        parts = []
        for t in range(share):
            one = product_parts(second, earlier[t])
            two = product_parts(third, earliest[t])
            upper, mid, lower = [a + b for a, b in zip(one, two)]
            parts.append(near(upper) * 15.0 + near(mid) * 256.0 + lower)
        if step:
            inverting.advance(16)

        wait_in(incoming.at[step, pl.ds(0, half)], block_sem.at[half])
        applied = []
        for t in range(share):
            total = outgoing[step, my_row * share + t]
            for m in [0] + list(range(half + 1, n_row)):
                total = total + incoming[step, m, t]
            applied.append(near(total))

        if step == 0:
            ready = [near(applied[t] + parts[t]) for t in range(share)]
            for t in range(share):
                full_b[my_row * share + t] = ready[t]
            gather_start(1, full_b)
            square_rows(applied)
            inverting.advance(14)
            for m in range(1, half):
                gather_pass(1, full_b, m)
                inverting.advance(6)
            inverse_now = inverting.result()
            square_cols()
            gather_end(full_b)
            forward(1, full_b)
            square_now = square_end()
            first = near(
                identity - small_product(near(square_now + gram_now), inverse_now)
            )
            rest = [fold_three(*product_parts(first, projected[r])) for r in range(tile_rows)]
            following = []
            for t in range(share):
                upper, mid, lower = product_parts(first, current[t])
                following.append(
                    whole(ready[t] + near(upper) * 15.0 + near(mid) * 256.0 + lower)
                )
                next_ref[:, t * size : (t + 1) * size] = following[t]
            next_out = pltpu.make_async_copy(next_ref, next_hbm, local_sem.at[0])
            next_out.start()
            partial_end(1)
            projected = [near(summed_partial(1, r) + rest[r]) for r in range(tile_rows)]
            earliest, earlier, current = earlier, current, [near(f) for f in following]
            inverse_older, inverse_old = inverse_old, inverse_now
            gram_old, square_old = gram_now, square_now
            continue

        if direct:
            square_direct(applied)
        else:
            square_rows(applied)
        inverse_now = inverting.result()
        turned = [small_product(inverse_now, current[t]) for t in range(share)]
        before = []
        for t in range(share):
            upper, mid, lower = product_parts(gram_now, turned[t])
            done = near(upper) * 15.0 + near(mid) * 256.0 + lower
            before.append(near(near(applied[t] + parts[t]) + current[t] - done))
        if direct:
            others = square_all.at[pl.ds(0, n_row * n_col - 1)]
            wait_in(others, recv_sem.at[SQUARE_ALL_IN])
            wait_out(others, SQUARE_ALL_OUT)
            square_now = unpack(summed(square_all, n_row * n_col))
        else:
            square_cols()
            square_now = square_end()
        for t in range(share):
            upper, mid, lower = product_parts(square_now, turned[t])
            done = near(upper) * 15.0 + near(mid) * 256.0 + lower
            later_ref[:, t * size : (t + 1) * size] = whole(before[t] - done)
        later_out = pltpu.make_async_copy(later_ref, later_hbm, local_sem.at[1])
        later_out.start()

    for step in range(2):
        wait_out(outgoing.at[:, pl.ds(0, (n_row - 1) * share)], BLOCKS_OUT + step)
        wait_out(partial.at[step, pl.ds(0, n_col - 1)], PARTIAL_OUT + step)
    next_out.wait()
    later_out.wait()


def body(
    n_row, n_col, entries, tile_cols, block_now, block_prev, block_prev2,
    gram_prev, square_prev, inverse_prev, inverse_prev2,
):
    tile_rows, slots, size = entries.shape[:3]
    order, width = block_now.shape
    share = width // size
    col_tiles = n_row * share
    stored = tile_rows * slots
    assert tile_rows <= 4 and share <= 4 and n_row % 2 == 0

    f32 = jnp.float32
    smem = pl.BlockSpec(memory_space=pltpu.SMEM)
    anywhere = pl.BlockSpec(memory_space=pl.ANY)
    devices = n_row * n_col if direct_squares(n_row, n_col) else 1
    packed = (order // 4, order * 4)
    following, later = pl.pallas_call(
        functools.partial(kernel, n_row, n_col),
        out_shape=(jax.ShapeDtypeStruct((order, width), f32),) * 2,
        in_specs=[smem] + [anywhere] * 8,
        out_specs=(anywhere, anywhere),
        scratch_shapes=[
            pltpu.VMEM(entries.shape, jnp.int32),
            pltpu.VMEM((order, width), jnp.int32),
            pltpu.VMEM((2, order, width), jnp.int32),
            pltpu.VMEM((4, order, order), jnp.int32),
            *[pltpu.VMEM((order, width), f32)] * 2,
            pltpu.VMEM((stored, size, size), jnp.bfloat16),
            pltpu.VMEM((col_tiles, order, size), f32),
            pltpu.VMEM((col_tiles, order, size), f32),
            pltpu.VMEM((2, n_col, tile_rows, order, size), f32),
            pltpu.VMEM((stored, 2 * order, size), f32),
            pltpu.VMEM((stored + 1, 2 * order, size), f32),
            pltpu.VMEM((2, col_tiles, order, size), f32),
            pltpu.VMEM((2, n_row, share, order, size), f32),
            pltpu.VMEM((2, n_row) + packed, f32),
            pltpu.VMEM((n_row,) + packed, f32),
            pltpu.VMEM((n_col,) + packed, f32),
            pltpu.VMEM((devices,) + packed, f32),
            pltpu.SMEM((stored,), jnp.int32),
            pltpu.SMEM((col_tiles + 1,), jnp.int32),
            pltpu.SemaphoreType.DMA((4,)),
            pltpu.SemaphoreType.DMA((8,)),
            pltpu.SemaphoreType.DMA((6,)),
            pltpu.SemaphoreType.DMA((n_row,)),
            pltpu.SemaphoreType.REGULAR,
        ],
        compiler_params=pltpu.CompilerParams(collective_id=0, has_side_effects=True),
    )(
        tile_cols, entries, block_now, block_prev, block_prev2,
        gram_prev, square_prev, inverse_prev, inverse_prev2,
    )
    return following / modulus, later / modulus


def solution(mesh):
    placed = (
        P("row", "col", None, None),
        P("row", "col"),
        P(None, ("col", "row")),
        P(None, ("col", "row")),
        P(None, ("col", "row")),
        P(),
        P(),
        P(),
        P(),
    )
    return jax.shard_map(
        functools.partial(body, mesh.shape["row"], mesh.shape["col"]),
        mesh=mesh,
        in_specs=placed,
        out_specs=(P(None, ("col", "row")), P(None, ("col", "row"))),
        check_vma=False,
    )
```

```python
import functools

import jax
import jax.numpy as jnp
from jax import lax
from jax.experimental import pallas as pl
from jax.experimental.pallas import tpu as pltpu
from jax.sharding import PartitionSpec as P

modulus = 65521.0
reciprocal = 1.0 / 65521.0
MESH = pl.DeviceIdType.MESH
GROUPS = 2
BLOCKS_OUT, PARTIAL_OUT, GRAM_OUT, SQUARE_ROW_OUT, SQUARE_COL_OUT, SQUARE_ALL_OUT = 0, 2, 4, 5, 6, 7
GRAM_IN, SQUARE_ROW_IN, SQUARE_COL_IN, SQUARE_ALL_IN = 0, 1, 2, 3


def near(values):
    return values - jnp.floor(values * reciprocal + 0.5) * modulus


def whole(values):
    signed = near(values)
    return jnp.where(signed < 0.0, signed + modulus, signed)


def split(values):
    top = jnp.floor(values * (1.0 / 256.0) + 0.5)
    return top, values - top * 256.0


def digits(values):
    top, low = split(values)
    return jnp.concatenate([top, low], axis=0).astype(jnp.bfloat16)


def fold_two(top, low):
    return near(near(top) * 256.0 + low)


def fold_three(upper, middle, lower):
    return near(near(upper) * 15.0 + near(middle) * 256.0 + near(lower))


def mulmod(left, right):
    top, low = split(right)
    return near(near(left * top) * 256.0 + left * low)


def dot(left, right):
    return jnp.dot(left, right, preferred_element_type=jnp.float32)


def dot_t(left, right):
    return lax.dot_general(
        left, right, (((1,), (1,)), ((), ())), preferred_element_type=jnp.float32
    )


def product_parts(left, right):
    order = left.shape[0]
    left_digits = digits(left)
    right_top, right_low = split(right)
    with_top = dot(left_digits, right_top.astype(jnp.bfloat16))
    with_low = dot(left_digits, right_low.astype(jnp.bfloat16))
    return with_top[:order], with_top[order:] + with_low[:order], with_low[order:]


def small_product(left, right):
    return fold_three(*product_parts(left, right))


def gram_tiles(tiles):
    order = tiles[0].shape[0]
    total = None
    for tile in tiles:
        both = digits(tile)
        term = dot_t(both, both)
        total = term if total is None else total + term
    return fold_three(
        total[:order, :order],
        total[:order, order:] + total[order:, :order],
        total[order:, order:],
    )


def power_inverse(number):
    result = None
    square = number
    for position in range(16):
        if 65519 >> position & 1:
            result = square if result is None else mulmod(result, square)
        if position < 15:
            square = mulmod(square, square)
    return result


def identity_of(order):
    rows = lax.broadcasted_iota(jnp.int32, (order, order), 0)
    lanes = lax.broadcasted_iota(jnp.int32, (order, order), 1)
    return jnp.where(rows == lanes, 1.0, 0.0).astype(jnp.float32)


class Elimination:
    def __init__(self, matrix):
        self.order = matrix.shape[0]
        self.done = 0
        self.work = jnp.concatenate([matrix, identity_of(self.order)], axis=1)

    def advance(self, columns):
        last = min(self.order, self.done + columns)
        for column in range(self.done, last):
            self.work = eliminated(self.work, column)
        self.done = last

    def result(self):
        self.advance(self.order)
        left = self.work[:, : self.order]
        diagonal = jnp.sum(left * identity_of(self.order), axis=1, keepdims=True)
        return mulmod(self.work[:, self.order :], power_inverse(diagonal))


def eliminated(work, column):
    order = work.shape[0]
    rows = lax.broadcasted_iota(jnp.int32, (order, 1), 0)
    entry = work[:, column : column + 1]
    usable = (entry != 0.0) & (rows >= column)
    first = jnp.min(jnp.where(usable, rows, order), axis=0, keepdims=True)
    chosen = rows == jnp.where(first == order, column, first)
    pivot_row = jnp.sum(jnp.where(chosen, work, 0.0), axis=0, keepdims=True)
    pivot = jnp.sum(jnp.where(chosen, entry, 0.0), axis=0, keepdims=True)
    swapped = jnp.where(chosen, work[column : column + 1, :], work)
    factor = jnp.where(chosen, entry[column : column + 1, :], entry)
    pivot_row = jnp.where(pivot == 0.0, 0.0, pivot_row)
    pivot = jnp.where(pivot == 0.0, 1.0, pivot)
    pivot_top, pivot_low = split(pivot)
    factor_top, factor_low = split(factor)
    upper = near(pivot_top * swapped - factor_top * pivot_row)
    reduced = near(upper * 256.0 + (pivot_low * swapped - factor_low * pivot_row))
    return jnp.where(rows == column, pivot_row, reduced)


def pack(values):
    rows = values.shape[0] // 4
    return jnp.concatenate([values[g * rows : (g + 1) * rows] for g in range(4)], axis=1)


def unpack(values):
    width = values.shape[1] // 4
    return jnp.concatenate([values[:, g * width : (g + 1) * width] for g in range(4)], axis=0)


def direct_squares(n_row, n_col):
    return n_row * n_col <= 64


def flipped(place, mask, count):
    assert count & (count - 1) == 0
    bit = 1
    moved = place
    while bit < count:
        if mask & bit:
            moved = moved + bit - 2 * bit * lax.rem(place // bit, 2)
        bit *= 2
    return moved


def kernel(
    n_row, n_col, cols_ref,
    entries_hbm, now_hbm, prev_hbm, prev2_hbm,
    gram_hbm, square_hbm, inverse_hbm, inverse2_hbm, next_hbm, later_hbm,
    entries_ref, now_ref, older_ref, small_ref, next_ref, later_ref,
    tile16, full_a, full_b, partial, spread, running, outgoing, incoming,
    gram_buf, square_row, square_col, square_all, order_ref, begin_ref,
    local_sem, send_sem, recv_sem, block_sem, partial_sem, fence_sem,
):
    my_row = lax.axis_index("row")
    my_col = lax.axis_index("col")
    tile_rows, slots, size = entries_ref.shape[:3]
    stored = tile_rows * slots
    order = now_ref.shape[0]
    share = now_ref.shape[1] // size
    half = n_row // 2
    rows = order // GROUPS
    direct = direct_squares(n_row, n_col)

    def row_peer(m):
        return flipped(my_row, m, n_row)

    def col_peer(m):
        return flipped(my_col, m, n_col)

    arrivals = [(now_hbm, now_ref, 0), (entries_hbm, entries_ref, 1)]
    arrivals += [(prev_hbm, older_ref.at[0], 2), (prev2_hbm, older_ref.at[1], 2)]
    for i, source in enumerate([gram_hbm, square_hbm, inverse_hbm, inverse2_hbm]):
        arrivals.append((source, small_ref.at[i], 3))
    copies_in = [
        pltpu.make_async_copy(source, target, local_sem.at[i]) for source, target, i in arrivals
    ]

    def local_wait(ref, i):
        pltpu.make_async_copy(ref, ref, local_sem.at[i]).wait()

    pairs = [(m, k) for k in range(n_col) for m in range(n_row) if m or k]
    if not direct:
        pairs = [(m, k) for m, k in pairs if m == 0 or k == 0]
    copies_in[0].start()
    barrier = pltpu.get_barrier_semaphore()
    for m, k in pairs:
        pl.semaphore_signal(
            barrier, inc=1, device_id=(row_peer(m), col_peer(k)), device_id_type=MESH
        )
    for copy in copies_in[1:]:
        copy.start()

    def remote(source, target, out, into, device):
        return pltpu.make_async_remote_copy(
            src_ref=source, dst_ref=target, send_sem=out, recv_sem=into,
            device_id=device, device_id_type=MESH,
        )

    def send(source, target, out, into, device):
        copy = remote(source, target, send_sem.at[out], into, device)
        copy.start()
        return copy

    def fence():
        pl.semaphore_signal(fence_sem, 1)
        pl.semaphore_wait(fence_sem, 1)

    def wait_in(ref, into):
        remote(ref, ref, send_sem.at[0], into, (my_row, my_col)).wait_recv()

    def wait_out(ref, out):
        remote(ref, ref, send_sem.at[out], recv_sem.at[0], (my_row, my_col)).wait_send()

    def tiles_of(values):
        return [values[:, t * size : (t + 1) * size] for t in range(share)]

    def load(ref):
        return tiles_of(near(ref[...].astype(jnp.float32)))

    def block(full, row):
        return full.at[pl.ds(row * share, share)]

    def joined(groups):
        return [jnp.concatenate([g[t] for g in groups], axis=0) for t in range(len(groups[0]))]

    def part(values, h):
        return values[h * rows : (h + 1) * rows]

    local_wait(now_ref, 0)
    current = load(now_ref)
    for h in range(GROUPS):
        for t in range(share):
            full_a[h][my_row * share + t] = part(current[t], h)
    pl.semaphore_wait(barrier, len(pairs))

    def gather_start(step, h, full):
        mine = block(full[h], my_row)
        for m in range(1, half):
            send(mine, mine, BLOCKS_OUT + step, block_sem.at[h, m], (row_peer(2 * m), my_col))
        send(mine, mine, BLOCKS_OUT + step, block_sem.at[h, 0], (row_peer(1), my_col))
        fence()

    def gather_pass(step, h, full, m):
        got = block(full[h], row_peer(2 * m))
        wait_in(got, block_sem.at[h, m])
        send(got, got, BLOCKS_OUT + step, block_sem.at[h, 0], (row_peer(1), my_col))
        fence()

    def gather_end(h, full):
        wait_in(full[h].at[pl.ds(0, half * share)], block_sem.at[h, 0])

    def third_of():
        middle = near(identity - small_product(inverse_old, gram_old))
        return -small_product(
            small_product(near(square_old + gram_old), middle), inverse_older
        )

    gather_start(0, 0, full_a)
    local_wait(entries_ref, 1)
    for i in range(stored):
        tile16[i] = entries_ref[i // slots, i % slots].astype(jnp.float32).astype(jnp.bfloat16)
    fence()
    for h in range(1, GROUPS):
        gather_start(0, h, full_a)
    local_wait(older_ref, 2)
    local_wait(small_ref, 3)
    earlier, earliest = load(older_ref.at[0]), load(older_ref.at[1])
    gram_old = near(small_ref[0].astype(jnp.float32))
    square_old = near(small_ref[1].astype(jnp.float32))
    inverse_old = near(small_ref[2].astype(jnp.float32))
    inverse_older = near(small_ref[3].astype(jnp.float32))
    identity = identity_of(order)
    cols = [cols_ref[i // slots, i % slots] for i in range(stored)]

    def as_int(flag):
        return jnp.where(flag, 1, 0).astype(jnp.int32)

    third = third_of()

    def rank_all():
        ranks = []
        for i in range(stored):
            rank = jnp.int32(0)
            for j in range(stored):
                if j != i:
                    rank = rank + as_int(cols[j] <= cols[i] if j < i else cols[j] < cols[i])
            ranks.append(rank)
        for k in range(stored):
            place = jnp.int32(0)
            for i in range(1, stored):
                place = place + jnp.where(ranks[i] == k, i, 0).astype(jnp.int32)
            order_ref[k] = place

    def count(tile, carry):
        below = jnp.int32(0)
        for i in range(stored):
            below = below + as_int(cols[i] < tile)
        begin_ref[tile] = below
        return carry

    for h in range(GROUPS):
        for m in range(1, half):
            gather_pass(0, h, full_a, m)
            if h == 0 and m == 1:
                rank_all()
    lax.fori_loop(0, n_row * share + 1, count, 0)

    def forward(step, h, full):
        for r in range(tile_rows):
            total = None
            for s in range(slots):
                picked = full[h][cols[r * slots + s]]
                term = dot_t(digits(picked), tile16[r * slots + s])
                total = term if total is None else total + term
            partial[step, h, my_col, r] = fold_two(total[:rows], total[rows:])
            own = partial.at[step, h, my_col, r]
            for m in range(1, n_col):
                send(
                    own, own, PARTIAL_OUT + step, partial_sem.at[step, h],
                    (my_row, col_peer(m)),
                )
            fence()

    def partial_end(step, h):
        wait_in(partial.at[step, h, pl.ds(0, n_col - 1)], partial_sem.at[step, h])
        sums = []
        for r in range(tile_rows):
            total = partial[step, h, 0, r]
            for c in range(1, n_col):
                total = total + partial[step, h, c, r]
            sums.append(total)
        return sums

    for h in range(GROUPS):
        gather_end(h, full_a)
        forward(0, h, full_a)

    def summed(buffer, count):
        total = buffer[0]
        for r in range(1, count):
            total = total + buffer[r]
        return near(total)

    def to_row(buffer, out, into):
        own = buffer.at[my_row]
        for m in range(1, n_row):
            send(own, own, out, recv_sem.at[into], (row_peer(m), my_col))
        fence()

    def from_row(buffer, out, into):
        others = buffer.at[pl.ds(0, n_row - 1)]
        wait_in(others, recv_sem.at[into])
        wait_out(others, out)
        return summed(buffer, n_row)

    def square_start(step, applied):
        packed = pack(gram_tiles(joined(applied)))
        if direct:
            mine = my_row * n_col + my_col
            square_all[step, mine] = packed
            own = square_all.at[step, mine]
            for m, k in reversed(pairs):
                send(
                    own, own, SQUARE_ALL_OUT, recv_sem.at[SQUARE_ALL_IN + step],
                    (row_peer(m), col_peer(k)),
                )
            fence()
        else:
            square_row[my_row] = packed
            to_row(square_row, SQUARE_ROW_OUT, SQUARE_ROW_IN)

    def square_cols():
        if direct:
            return
        square_col[my_col] = from_row(square_row, SQUARE_ROW_OUT, SQUARE_ROW_IN)
        own = square_col.at[my_col]
        for m in range(1, n_col):
            send(own, own, SQUARE_COL_OUT, recv_sem.at[SQUARE_COL_IN], (my_row, col_peer(m)))
        fence()

    def square_end(step):
        if direct:
            others = square_all.at[step, pl.ds(0, n_row * n_col - 1)]
            wait_in(others, recv_sem.at[SQUARE_ALL_IN + step])
            wait_out(others, SQUARE_ALL_OUT)
            return unpack(summed(square_all.at[step], n_row * n_col))
        others = square_col.at[pl.ds(0, n_col - 1)]
        wait_in(others, recv_sem.at[SQUARE_COL_IN])
        wait_out(others, SQUARE_COL_OUT)
        return unpack(summed(square_col, n_col))

    def spread_out(step, h, projected):
        for r in range(tile_rows):
            both = digits(projected[r])
            for s in range(slots):
                spread[h, r * slots + s] = dot(both, tile16[r * slots + s])
        total = jnp.zeros((2 * rows, size), jnp.float32)
        running[h, 0] = total
        for i in range(stored):
            total = total + spread[h, order_ref[i]]
            running[h, i + 1] = total

        def finish_block(peer):
            for t in range(share):
                tile = peer * share + t
                sums = running[h, begin_ref[tile + 1]] - running[h, begin_ref[tile]]
                outgoing[step, h, tile] = fold_two(sums[:rows], sums[rows:])

        for m in range(half - 1, -1, -1):
            peer = row_peer(2 * m + 1)
            finish_block(peer)
            send(
                block(outgoing.at[step, h], peer), incoming.at[step, h, m],
                BLOCKS_OUT + step, block_sem.at[h, half + m], (row_peer(1), my_col),
            )
            fence()
        for m in range(half - 1, -1, -1):
            finish_block(row_peer(2 * m))

    def scatter_pass(step, h, m):
        wait_in(incoming.at[step, h, m], block_sem.at[h, half + m])
        peer = row_peer(2 * m)
        for t in range(share):
            outgoing[step, h, peer * share + t] = (
                outgoing[step, h, peer * share + t] + incoming[step, h, m, t]
            )
        send(
            block(outgoing.at[step, h], peer), incoming.at[step, h, half + m],
            BLOCKS_OUT + step, block_sem.at[h, half], (peer, my_col),
        )
        fence()

    def scatter_end(step, h):
        wait_in(incoming.at[step, h, pl.ds(0, half)], block_sem.at[h, half])
        applied = []
        for t in range(share):
            total = outgoing[step, h, my_row * share + t]
            for m in [0] + list(range(half + 1, n_row)):
                total = total + incoming[step, h, m, t]
            applied.append(near(total))
        return applied

    rest = None
    for step in range(2):
        projected = []
        for h in range(GROUPS):
            sums = partial_end(step, h)
            if step:
                if h == 0:
                    square_now = square_end(0)
                    first = near(
                        identity - small_product(near(square_now + gram_now), inverse_now)
                    )
                    rest = [fold_three(*product_parts(first, y)) for y in joined(before)]
                sums = [sums[r] + part(rest[r], h) for r in range(tile_rows)]
            projected.append([near(total) for total in sums])
            spread_out(step, h, projected[h])
        before = projected
        gram_buf[step, my_row] = pack(gram_tiles(joined(projected)))
        to_row(gram_buf.at[step], GRAM_OUT, GRAM_IN)
        if step:
            following = []
            for t in range(share):
                upper, mid, lower = product_parts(first, current[t])
                following.append(
                    whole(ready[t] + near(upper) * 15.0 + near(mid) * 256.0 + lower)
                )
                next_ref[:, t * size : (t + 1) * size] = following[t]
            next_out = pltpu.make_async_copy(next_ref, next_hbm, local_sem.at[0])
            next_out.start()
            earliest, earlier, current = earlier, current, [near(f) for f in following]
            inverse_older, inverse_old = inverse_old, inverse_now
            gram_old, square_old = gram_now, square_now
            third = third_of()
            fence()
        for h in range(GROUPS):
            for m in range(half - 1, 0, -1):
                scatter_pass(step, h, m)

        gram_now = unpack(from_row(gram_buf.at[step], GRAM_OUT, GRAM_IN))
        inverting = Elimination(gram_now)
        second = -small_product(gram_now, inverse_old)
        parts = []
        for t in range(share):
            one = product_parts(second, earlier[t])
            two = product_parts(third, earliest[t])
            upper, mid, lower = [a + b for a, b in zip(one, two)]
            parts.append(near(upper) * 15.0 + near(mid) * 256.0 + lower)

        applied = []
        for h in range(GROUPS):
            if step:
                inverting.advance(8)
            applied.append(scatter_end(step, h))
            if step == 0:
                for t in range(share):
                    full_b[h][my_row * share + t] = near(applied[h][t] + part(parts[t], h))
                gather_start(1, h, full_b)
        ready = [near(a + b) for a, b in zip(joined(applied), parts)]
        square_start(step, applied)

        if step == 0:
            inverting.advance(4)
            for h in range(GROUPS):
                for m in range(1, half):
                    gather_pass(1, h, full_b, m)
                    inverting.advance(5)
            inverse_now = inverting.result()
            square_cols()
            for h in range(GROUPS):
                gather_end(h, full_b)
                forward(1, h, full_b)
            continue

        inverse_now = inverting.result()
        turned = [small_product(inverse_now, current[t]) for t in range(share)]
        fixed = []
        for t in range(share):
            upper, mid, lower = product_parts(gram_now, turned[t])
            done = near(upper) * 15.0 + near(mid) * 256.0 + lower
            fixed.append(near(ready[t] + current[t] - done))
        square_cols()
        square_now = square_end(1)
        for t in range(share):
            upper, mid, lower = product_parts(square_now, turned[t])
            done = near(upper) * 15.0 + near(mid) * 256.0 + lower
            later_ref[:, t * size : (t + 1) * size] = whole(fixed[t] - done)
        later_out = pltpu.make_async_copy(later_ref, later_hbm, local_sem.at[1])
        later_out.start()

    for step in range(2):
        wait_out(outgoing.at[:, :, pl.ds(0, (n_row - 1) * share)], BLOCKS_OUT + step)
        wait_out(partial.at[step, :, pl.ds(0, n_col - 1)], PARTIAL_OUT + step)
    next_out.wait()
    later_out.wait()


def body(
    n_row, n_col, entries, tile_cols, block_now, block_prev, block_prev2,
    gram_prev, square_prev, inverse_prev, inverse_prev2,
):
    tile_rows, slots, size = entries.shape[:3]
    order, width = block_now.shape
    share = width // size
    col_tiles = n_row * share
    stored = tile_rows * slots
    rows = order // GROUPS
    assert order % (8 * GROUPS) == 0
    assert tile_rows <= 4 and share <= 4 and n_row % 2 == 0

    f32 = jnp.float32
    smem = pl.BlockSpec(memory_space=pltpu.SMEM)
    anywhere = pl.BlockSpec(memory_space=pl.ANY)
    devices = n_row * n_col if direct_squares(n_row, n_col) else 1
    packed = (order // 4, order * 4)
    following, later = pl.pallas_call(
        functools.partial(kernel, n_row, n_col),
        out_shape=(jax.ShapeDtypeStruct((order, width), f32),) * 2,
        in_specs=[smem] + [anywhere] * 8,
        out_specs=(anywhere, anywhere),
        scratch_shapes=[
            pltpu.VMEM(entries.shape, jnp.int32),
            pltpu.VMEM((order, width), jnp.int32),
            pltpu.VMEM((2, order, width), jnp.int32),
            pltpu.VMEM((4, order, order), jnp.int32),
            *[pltpu.VMEM((order, width), f32)] * 2,
            pltpu.VMEM((stored, size, size), jnp.bfloat16),
            [pltpu.VMEM((col_tiles, rows, size), f32)] * GROUPS,
            [pltpu.VMEM((col_tiles, rows, size), f32)] * GROUPS,
            pltpu.VMEM((2, GROUPS, n_col, tile_rows, rows, size), f32),
            pltpu.VMEM((GROUPS, stored, 2 * rows, size), f32),
            pltpu.VMEM((GROUPS, stored + 1, 2 * rows, size), f32),
            pltpu.VMEM((2, GROUPS, col_tiles, rows, size), f32),
            pltpu.VMEM((2, GROUPS, n_row, share, rows, size), f32),
            pltpu.VMEM((2, n_row) + packed, f32),
            pltpu.VMEM((n_row,) + packed, f32),
            pltpu.VMEM((n_col,) + packed, f32),
            pltpu.VMEM((2, devices) + packed, f32),
            pltpu.SMEM((stored,), jnp.int32),
            pltpu.SMEM((col_tiles + 1,), jnp.int32),
            pltpu.SemaphoreType.DMA((4,)),
            pltpu.SemaphoreType.DMA((8,)),
            pltpu.SemaphoreType.DMA((5,)),
            pltpu.SemaphoreType.DMA((GROUPS, n_row)),
            pltpu.SemaphoreType.DMA((2, GROUPS)),
            pltpu.SemaphoreType.REGULAR,
        ],
        compiler_params=pltpu.CompilerParams(collective_id=0, has_side_effects=True),
    )(
        tile_cols, entries, block_now, block_prev, block_prev2,
        gram_prev, square_prev, inverse_prev, inverse_prev2,
    )
    return following / modulus, later / modulus


def solution(mesh):
    placed = (
        P("row", "col", None, None),
        P("row", "col"),
        P(None, ("col", "row")),
        P(None, ("col", "row")),
        P(None, ("col", "row")),
        P(),
        P(),
        P(),
        P(),
    )
    return jax.shard_map(
        functools.partial(body, mesh.shape["row"], mesh.shape["col"]),
        mesh=mesh,
        in_specs=placed,
        out_specs=(P(None, ("col", "row")), P(None, ("col", "row"))),
        check_vma=False,
    )
```

```python
import functools

import jax
import jax.numpy as jnp
from jax import lax
from jax.experimental import pallas as pl
from jax.experimental.pallas import tpu as pltpu
from jax.sharding import PartitionSpec as P

modulus = 65521.0
reciprocal = 1.0 / 65521.0
MESH = pl.DeviceIdType.MESH
GROUPS = 2
BLOCKS_OUT, PARTIAL_OUT, GRAM_OUT, SQUARE_ROW_OUT, SQUARE_COL_OUT, SQUARE_ALL_OUT = 0, 2, 4, 5, 6, 7
GRAM_IN, SQUARE_ROW_IN, SQUARE_COL_IN, SQUARE_ALL_IN = 0, 1, 2, 3


def near(values):
    return values - jnp.floor(values * reciprocal + 0.5) * modulus


def whole(values):
    signed = near(values)
    return jnp.where(signed < 0.0, signed + modulus, signed)


def split(values):
    top = jnp.floor(values * (1.0 / 256.0) + 0.5)
    return top, values - top * 256.0


def digits(values):
    top, low = split(values)
    return jnp.concatenate([top, low], axis=0).astype(jnp.bfloat16)


def fold_two(top, low):
    return near(near(top) * 256.0 + low)


def fold_three(upper, middle, lower):
    return near(near(upper) * 15.0 + near(middle) * 256.0 + near(lower))


def mulmod(left, right):
    top, low = split(right)
    return near(near(left * top) * 256.0 + left * low)


def dot(left, right):
    return jnp.dot(left, right, preferred_element_type=jnp.float32)


def dot_t(left, right):
    return lax.dot_general(
        left, right, (((1,), (1,)), ((), ())), preferred_element_type=jnp.float32
    )


def product_parts(left, right):
    order = left.shape[0]
    left_digits = digits(left)
    right_top, right_low = split(right)
    with_top = dot(left_digits, right_top.astype(jnp.bfloat16))
    with_low = dot(left_digits, right_low.astype(jnp.bfloat16))
    return with_top[:order], with_top[order:] + with_low[:order], with_low[order:]


def small_product(left, right):
    return fold_three(*product_parts(left, right))


def gram_tiles(tiles):
    order = tiles[0].shape[0]
    total = None
    for tile in tiles:
        both = digits(tile)
        term = dot_t(both, both)
        total = term if total is None else total + term
    return fold_three(
        total[:order, :order],
        total[:order, order:] + total[order:, :order],
        total[order:, order:],
    )


def power_inverse(number):
    result = None
    square = number
    for position in range(16):
        if 65519 >> position & 1:
            result = square if result is None else mulmod(result, square)
        if position < 15:
            square = mulmod(square, square)
    return result


def identity_of(order):
    rows = lax.broadcasted_iota(jnp.int32, (order, order), 0)
    lanes = lax.broadcasted_iota(jnp.int32, (order, order), 1)
    return jnp.where(rows == lanes, 1.0, 0.0).astype(jnp.float32)


class Elimination:
    def __init__(self, matrix):
        self.order = matrix.shape[0]
        self.done = 0
        self.work = jnp.concatenate([matrix, identity_of(self.order)], axis=1)

    def advance(self, columns):
        last = min(self.order, self.done + columns)
        for column in range(self.done, last):
            self.work = eliminated(self.work, column)
        self.done = last

    def result(self):
        self.advance(self.order)
        left = self.work[:, : self.order]
        diagonal = jnp.sum(left * identity_of(self.order), axis=1, keepdims=True)
        return mulmod(self.work[:, self.order :], power_inverse(diagonal))


def eliminated(work, column):
    order = work.shape[0]
    rows = lax.broadcasted_iota(jnp.int32, (order, 1), 0)
    entry = work[:, column : column + 1]
    usable = (entry != 0.0) & (rows >= column)
    first = jnp.min(jnp.where(usable, rows, order), axis=0, keepdims=True)
    chosen = rows == jnp.where(first == order, column, first)
    pivot_row = jnp.sum(jnp.where(chosen, work, 0.0), axis=0, keepdims=True)
    pivot = jnp.sum(jnp.where(chosen, entry, 0.0), axis=0, keepdims=True)
    swapped = jnp.where(chosen, work[column : column + 1, :], work)
    factor = jnp.where(chosen, entry[column : column + 1, :], entry)
    pivot_row = jnp.where(pivot == 0.0, 0.0, pivot_row)
    pivot = jnp.where(pivot == 0.0, 1.0, pivot)
    pivot_top, pivot_low = split(pivot)
    factor_top, factor_low = split(factor)
    upper = near(pivot_top * swapped - factor_top * pivot_row)
    reduced = near(upper * 256.0 + (pivot_low * swapped - factor_low * pivot_row))
    return jnp.where(rows == column, pivot_row, reduced)


def pack(values):
    rows = values.shape[0] // 4
    return jnp.concatenate([values[g * rows : (g + 1) * rows] for g in range(4)], axis=1)


def unpack(values):
    width = values.shape[1] // 4
    return jnp.concatenate([values[:, g * width : (g + 1) * width] for g in range(4)], axis=0)


def direct_squares(n_row, n_col):
    return n_row * n_col <= 64


def flipped(place, mask, count):
    assert count & (count - 1) == 0
    bit = 1
    moved = place
    while bit < count:
        if mask & bit:
            moved = moved + bit - 2 * bit * lax.rem(place // bit, 2)
        bit *= 2
    return moved


def kernel(
    n_row, n_col, cols_hbm,
    entries_hbm, now_hbm, prev_hbm, prev2_hbm,
    gram_hbm, square_hbm, inverse_hbm, inverse2_hbm, next_ref, later_ref,
    cols_ref, entries_ref, now_ref, older_ref, small_ref,
    tile16, tile_t, full_a, full_b, partial, spread, running, outgoing, incoming,
    gram_buf, square_row, square_col, square_all, order_ref, begin_ref,
    local_sem, send_sem, recv_sem, block_sem, partial_sem, fence_sem,
):
    my_row = lax.axis_index("row")
    my_col = lax.axis_index("col")
    tile_rows, slots, size = entries_ref.shape[:3]
    stored = tile_rows * slots
    order = now_ref.shape[0]
    share = now_ref.shape[1] // size
    half = n_row // 2
    rows = order // GROUPS
    direct = direct_squares(n_row, n_col)

    def row_peer(m):
        return flipped(my_row, m, n_row)

    def col_peer(m):
        return flipped(my_col, m, n_col)

    arrivals = [(now_hbm, now_ref, 0), (entries_hbm, entries_ref, 1)]
    arrivals += [(cols_hbm, cols_ref, 4), (prev_hbm, older_ref.at[0], 2), (prev2_hbm, older_ref.at[1], 2)]
    for i, source in enumerate([gram_hbm, square_hbm, inverse_hbm, inverse2_hbm]):
        arrivals.append((source, small_ref.at[i], 3))
    copies_in = [
        pltpu.make_async_copy(source, target, local_sem.at[i]) for source, target, i in arrivals
    ]

    def local_wait(ref, i):
        pltpu.make_async_copy(ref, ref, local_sem.at[i]).wait()

    pairs = [(m, k) for k in range(n_col) for m in range(n_row) if m or k]
    if not direct:
        pairs = [(m, k) for m, k in pairs if m == 0 or k == 0]
    copies_in[0].start()
    barrier = pltpu.get_barrier_semaphore()
    for m, k in pairs:
        pl.semaphore_signal(
            barrier, inc=1, device_id=(row_peer(m), col_peer(k)), device_id_type=MESH
        )
    for copy in copies_in[1:]:
        copy.start()

    def remote(source, target, out, into, device):
        return pltpu.make_async_remote_copy(
            src_ref=source, dst_ref=target, send_sem=out, recv_sem=into,
            device_id=device, device_id_type=MESH,
        )

    def send(source, target, out, into, device):
        copy = remote(source, target, send_sem.at[out], into, device)
        copy.start()
        return copy

    def fence():
        pl.semaphore_signal(fence_sem, 1)
        pl.semaphore_wait(fence_sem, 1)

    def wait_in(ref, into):
        remote(ref, ref, send_sem.at[0], into, (my_row, my_col)).wait_recv()

    def wait_out(ref, out):
        remote(ref, ref, send_sem.at[out], recv_sem.at[0], (my_row, my_col)).wait_send()

    def tiles_of(values):
        return [values[:, t * size : (t + 1) * size] for t in range(share)]

    def load(ref):
        return tiles_of(near(ref[...].astype(jnp.float32)))

    def block(full, row):
        return full.at[pl.ds(row * share, share)]

    def joined(groups):
        return [jnp.concatenate([g[t] for g in groups], axis=0) for t in range(len(groups[0]))]

    def part(values, h):
        return values[h * rows : (h + 1) * rows]

    local_wait(now_ref, 0)
    current = load(now_ref)
    for h in range(GROUPS):
        for t in range(share):
            full_a[h][my_row * share + t] = part(current[t], h)
    pl.semaphore_wait(barrier, len(pairs))

    def gather_start(step, h, full):
        mine = block(full[h], my_row)
        for m in range(1, half):
            send(mine, mine, BLOCKS_OUT + step, block_sem.at[h, m], (row_peer(2 * m), my_col))
        send(mine, mine, BLOCKS_OUT + step, block_sem.at[h, 0], (row_peer(1), my_col))
        fence()

    def gather_pass(step, h, full, m):
        got = block(full[h], row_peer(2 * m))
        wait_in(got, block_sem.at[h, m])
        send(got, got, BLOCKS_OUT + step, block_sem.at[h, 0], (row_peer(1), my_col))
        fence()

    def gather_end(h, full):
        wait_in(full[h].at[pl.ds(0, half * share)], block_sem.at[h, 0])

    def third_of():
        middle = near(identity - small_product(inverse_old, gram_old))
        return -small_product(
            small_product(near(square_old + gram_old), middle), inverse_older
        )

    gather_start(0, 0, full_a)
    local_wait(entries_ref, 1)
    for i in range(stored):
        tile16[i] = entries_ref[i // slots, i % slots].astype(jnp.float32).astype(jnp.bfloat16)
    fence()
    for h in range(1, GROUPS):
        gather_start(0, h, full_a)
    local_wait(older_ref, 2)
    local_wait(small_ref, 3)
    earlier, earliest = load(older_ref.at[0]), load(older_ref.at[1])
    gram_old = near(small_ref[0].astype(jnp.float32))
    square_old = near(small_ref[1].astype(jnp.float32))
    inverse_old = near(small_ref[2].astype(jnp.float32))
    inverse_older = near(small_ref[3].astype(jnp.float32))
    identity = identity_of(order)
    local_wait(cols_ref, 4)
    cols = [cols_ref[i // slots, i % slots] for i in range(stored)]

    def as_int(flag):
        return jnp.where(flag, 1, 0).astype(jnp.int32)

    third = third_of()

    def rank_all():
        ranks = []
        for i in range(stored):
            rank = jnp.int32(0)
            for j in range(stored):
                if j != i:
                    rank = rank + as_int(cols[j] <= cols[i] if j < i else cols[j] < cols[i])
            ranks.append(rank)
        for k in range(stored):
            place = jnp.int32(0)
            for i in range(1, stored):
                place = place + jnp.where(ranks[i] == k, i, 0).astype(jnp.int32)
            order_ref[k] = place

    def count(tile, carry):
        below = jnp.int32(0)
        for i in range(stored):
            below = below + as_int(cols[i] < tile)
        begin_ref[tile] = below
        return carry

    for i in range(stored):
        turned = entries_ref[i // slots, i % slots].astype(jnp.float32).T
        at = i % slots * size
        tile_t[i // slots, at : at + size] = turned.astype(jnp.bfloat16)
    lax.fori_loop(0, n_row * share + 1, count, 0)
    for h in range(GROUPS):
        for m in range(1, half):
            gather_pass(0, h, full_a, m)
    rank_all()

    def forward(step, h, full):
        for r in range(tile_rows):
            picked = [digits(full[h][cols[r * slots + s]]) for s in range(slots)]
            total = dot(jnp.concatenate(picked, axis=1), tile_t[r])
            partial[step, h, my_col, r] = fold_two(total[:rows], total[rows:])
            own = partial.at[step, h, my_col, r]
            for m in range(1, n_col):
                send(
                    own, own, PARTIAL_OUT + step, partial_sem.at[step, h],
                    (my_row, col_peer(m)),
                )
            fence()

    def partial_end(step, h):
        wait_in(partial.at[step, h, pl.ds(0, n_col - 1)], partial_sem.at[step, h])
        sums = []
        for r in range(tile_rows):
            total = partial[step, h, 0, r]
            for c in range(1, n_col):
                total = total + partial[step, h, c, r]
            sums.append(total)
        return sums

    for h in range(GROUPS):
        gather_end(h, full_a)
        forward(0, h, full_a)

    def summed(buffer, count):
        total = buffer[0]
        for r in range(1, count):
            total = total + buffer[r]
        return near(total)

    def to_row(buffer, out, into):
        own = buffer.at[my_row]
        for m in range(1, n_row):
            send(own, own, out, recv_sem.at[into], (row_peer(m), my_col))
        fence()

    def from_row(buffer, out, into):
        others = buffer.at[pl.ds(0, n_row - 1)]
        wait_in(others, recv_sem.at[into])
        wait_out(others, out)
        return summed(buffer, n_row)

    def square_start(step, applied):
        packed = pack(gram_tiles(joined(applied)))
        if direct:
            mine = my_row * n_col + my_col
            square_all[step, mine] = packed
            own = square_all.at[step, mine]
            for m, k in reversed(pairs):
                send(
                    own, own, SQUARE_ALL_OUT, recv_sem.at[SQUARE_ALL_IN + step],
                    (row_peer(m), col_peer(k)),
                )
            fence()
        else:
            square_row[my_row] = packed
            to_row(square_row, SQUARE_ROW_OUT, SQUARE_ROW_IN)

    def square_cols():
        if direct:
            return
        square_col[my_col] = from_row(square_row, SQUARE_ROW_OUT, SQUARE_ROW_IN)
        own = square_col.at[my_col]
        for m in range(1, n_col):
            send(own, own, SQUARE_COL_OUT, recv_sem.at[SQUARE_COL_IN], (my_row, col_peer(m)))
        fence()

    def square_end(step):
        if direct:
            others = square_all.at[step, pl.ds(0, n_row * n_col - 1)]
            wait_in(others, recv_sem.at[SQUARE_ALL_IN + step])
            wait_out(others, SQUARE_ALL_OUT)
            return unpack(summed(square_all.at[step], n_row * n_col))
        others = square_col.at[pl.ds(0, n_col - 1)]
        wait_in(others, recv_sem.at[SQUARE_COL_IN])
        wait_out(others, SQUARE_COL_OUT)
        return unpack(summed(square_col, n_col))

    def spread_out(step, h, projected):
        for r in range(tile_rows):
            both = digits(projected[r])
            for s in range(slots):
                spread[h, r * slots + s] = dot(both, tile16[r * slots + s])
        total = jnp.zeros((2 * rows, size), jnp.float32)
        running[h, 0] = total
        for i in range(stored):
            total = total + spread[h, order_ref[i]]
            running[h, i + 1] = total

        def finish_block(peer):
            for t in range(share):
                tile = peer * share + t
                sums = running[h, begin_ref[tile + 1]] - running[h, begin_ref[tile]]
                outgoing[step, h, tile] = fold_two(sums[:rows], sums[rows:])

        for m in range(half - 1, -1, -1):
            peer = row_peer(2 * m + 1)
            finish_block(peer)
            send(
                block(outgoing.at[step, h], peer), incoming.at[step, h, m],
                BLOCKS_OUT + step, block_sem.at[h, half + m], (row_peer(1), my_col),
            )
            fence()
        for m in range(half - 1, -1, -1):
            finish_block(row_peer(2 * m))

    def scatter_pass(step, h, m):
        wait_in(incoming.at[step, h, m], block_sem.at[h, half + m])
        peer = row_peer(2 * m)
        for t in range(share):
            outgoing[step, h, peer * share + t] = (
                outgoing[step, h, peer * share + t] + incoming[step, h, m, t]
            )
        send(
            block(outgoing.at[step, h], peer), incoming.at[step, h, half + m],
            BLOCKS_OUT + step, block_sem.at[h, half], (peer, my_col),
        )
        fence()

    def scatter_end(step, h):
        wait_in(incoming.at[step, h, pl.ds(0, half)], block_sem.at[h, half])
        applied = []
        for t in range(share):
            total = outgoing[step, h, my_row * share + t]
            for m in [0] + list(range(half + 1, n_row)):
                total = total + incoming[step, h, m, t]
            applied.append(near(total))
        return applied

    rest = None
    for step in range(2):
        projected = []
        if step:
            square_now = square_end(0)
            first = near(
                identity - small_product(near(square_now + gram_now), inverse_now)
            )
            rest = [fold_three(*product_parts(first, y)) for y in joined(before)]
        for h in range(GROUPS):
            sums = partial_end(step, h)
            if step:
                sums = [sums[r] + part(rest[r], h) for r in range(tile_rows)]
            projected.append([near(total) for total in sums])
            if h == GROUPS - 1:
                gram_buf[step, my_row] = pack(gram_tiles(joined(projected)))
                to_row(gram_buf.at[step], GRAM_OUT, GRAM_IN)
            spread_out(step, h, projected[h])
        before = projected
        if step:
            following = []
            for t in range(share):
                upper, mid, lower = product_parts(first, current[t])
                following.append(
                    whole(ready[t] + near(upper) * 15.0 + near(mid) * 256.0 + lower)
                )
                next_ref[:, t * size : (t + 1) * size] = following[t]
            earliest, earlier, current = earlier, current, [near(f) for f in following]
            inverse_older, inverse_old = inverse_old, inverse_now
            gram_old, square_old = gram_now, square_now
            third = third_of()
            fence()
        for h in range(GROUPS):
            for m in range(half - 1, 0, -1):
                scatter_pass(step, h, m)

        gram_now = unpack(from_row(gram_buf.at[step], GRAM_OUT, GRAM_IN))
        inverting = Elimination(gram_now)
        second = -small_product(gram_now, inverse_old)
        parts = []
        for t in range(share):
            one = product_parts(second, earlier[t])
            two = product_parts(third, earliest[t])
            upper, mid, lower = [a + b for a, b in zip(one, two)]
            parts.append(near(upper) * 15.0 + near(mid) * 256.0 + lower)

        applied = []
        for h in range(GROUPS):
            if step:
                inverting.advance(8)
            applied.append(scatter_end(step, h))
            if step == 0:
                for t in range(share):
                    full_b[h][my_row * share + t] = near(applied[h][t] + part(parts[t], h))
                gather_start(1, h, full_b)
        ready = [near(a + b) for a, b in zip(joined(applied), parts)]
        square_start(step, applied)

        if step == 0:
            inverting.advance(4)
            for h in range(GROUPS):
                for m in range(1, half):
                    gather_pass(1, h, full_b, m)
                    inverting.advance(4)
            square_cols()
            for h in range(GROUPS):
                gather_end(h, full_b)
                forward(1, h, full_b)
            inverse_now = inverting.result()
            continue

        inverse_now = inverting.result()
        turned = [small_product(inverse_now, current[t]) for t in range(share)]
        fixed = []
        for t in range(share):
            upper, mid, lower = product_parts(gram_now, turned[t])
            done = near(upper) * 15.0 + near(mid) * 256.0 + lower
            fixed.append(near(ready[t] + current[t] - done))
        square_cols()
        square_now = square_end(1)
        for t in range(share):
            upper, mid, lower = product_parts(square_now, turned[t])
            done = near(upper) * 15.0 + near(mid) * 256.0 + lower
            later_ref[:, t * size : (t + 1) * size] = whole(fixed[t] - done)

    for step in range(2):
        wait_out(outgoing.at[:, :, pl.ds(0, (n_row - 1) * share)], BLOCKS_OUT + step)
        wait_out(partial.at[step, :, pl.ds(0, n_col - 1)], PARTIAL_OUT + step)


def body(
    n_row, n_col, entries, tile_cols, block_now, block_prev, block_prev2,
    gram_prev, square_prev, inverse_prev, inverse_prev2,
):
    tile_rows, slots, size = entries.shape[:3]
    order, width = block_now.shape
    share = width // size
    col_tiles = n_row * share
    stored = tile_rows * slots
    rows = order // GROUPS
    assert order % (8 * GROUPS) == 0
    assert tile_rows <= 4 and share <= 4 and n_row % 2 == 0

    f32 = jnp.float32
    vmem = pl.BlockSpec(memory_space=pltpu.VMEM)
    hbm = pl.BlockSpec(memory_space=pltpu.HBM)
    devices = n_row * n_col if direct_squares(n_row, n_col) else 1
    packed = (order // 4, order * 4)
    following, later = pl.pallas_call(
        functools.partial(kernel, n_row, n_col),
        out_shape=(pltpu.VMEM((order, width), f32),) * 2,
        in_specs=[hbm] * 9,
        out_specs=(vmem, vmem),
        scratch_shapes=[
            pltpu.SMEM(tile_cols.shape, jnp.int32),
            pltpu.VMEM(entries.shape, jnp.int32),
            pltpu.VMEM((order, width), jnp.int32),
            pltpu.VMEM((2, order, width), jnp.int32),
            pltpu.VMEM((4, order, order), jnp.int32),
            pltpu.VMEM((stored, size, size), jnp.bfloat16),
            pltpu.VMEM((tile_rows, slots * size, size), jnp.bfloat16),
            [pltpu.VMEM((col_tiles, rows, size), f32)] * GROUPS,
            [pltpu.VMEM((col_tiles, rows, size), f32)] * GROUPS,
            pltpu.VMEM((2, GROUPS, n_col, tile_rows, rows, size), f32),
            pltpu.VMEM((GROUPS, stored, 2 * rows, size), f32),
            pltpu.VMEM((GROUPS, stored + 1, 2 * rows, size), f32),
            pltpu.VMEM((2, GROUPS, col_tiles, rows, size), f32),
            pltpu.VMEM((2, GROUPS, n_row, share, rows, size), f32),
            pltpu.VMEM((2, n_row) + packed, f32),
            pltpu.VMEM((n_row,) + packed, f32),
            pltpu.VMEM((n_col,) + packed, f32),
            pltpu.VMEM((2, devices) + packed, f32),
            pltpu.SMEM((stored,), jnp.int32),
            pltpu.SMEM((col_tiles + 1,), jnp.int32),
            pltpu.SemaphoreType.DMA((5,)),
            pltpu.SemaphoreType.DMA((8,)),
            pltpu.SemaphoreType.DMA((5,)),
            pltpu.SemaphoreType.DMA((GROUPS, n_row)),
            pltpu.SemaphoreType.DMA((2, GROUPS)),
            pltpu.SemaphoreType.REGULAR,
        ],
        compiler_params=pltpu.CompilerParams(collective_id=0, has_side_effects=True),
    )(
        tile_cols, entries, block_now, block_prev, block_prev2,
        gram_prev, square_prev, inverse_prev, inverse_prev2,
    )
    return following / modulus, later / modulus


def solution(mesh):
    placed = (
        P("row", "col", None, None),
        P("row", "col"),
        P(None, ("col", "row")),
        P(None, ("col", "row")),
        P(None, ("col", "row")),
        P(),
        P(),
        P(),
        P(),
    )
    return jax.shard_map(
        functools.partial(body, mesh.shape["row"], mesh.shape["col"]),
        mesh=mesh,
        in_specs=placed,
        out_specs=(P(None, ("col", "row")), P(None, ("col", "row"))),
        check_vma=False,
    )
```

```python
import functools

import jax
import jax.numpy as jnp
from jax import lax
from jax.experimental import pallas as pl
from jax.experimental.pallas import tpu as pltpu
from jax.sharding import PartitionSpec as P

modulus = 65521.0
reciprocal = 1.0 / 65521.0
MESH = pl.DeviceIdType.MESH
GROUPS = 4
LAG = 4
GRAM_TURN = 2
BLOCKS_OUT, PARTIAL_OUT, GRAM_OUT, SQUARE_ROW_OUT, SQUARE_COL_OUT, SQUARE_ALL_OUT = 0, 2, 4, 5, 6, 7
GRAM_IN, SQUARE_ROW_IN, SQUARE_COL_IN, SQUARE_ALL_IN = 0, 1, 2, 3


def near(values):
    return values - jnp.floor(values * reciprocal + 0.5) * modulus


def whole(values):
    signed = near(values)
    return jnp.where(signed < 0.0, signed + modulus, signed)


def split(values):
    top = jnp.floor(values * (1.0 / 256.0) + 0.5)
    return top, values - top * 256.0


def digits(values):
    top, low = split(values)
    return jnp.concatenate([top, low], axis=0).astype(jnp.bfloat16)


def fold_two(top, low):
    return near(near(top) * 256.0 + low)


def fold_three(upper, middle, lower):
    return near(near(upper) * 15.0 + near(middle) * 256.0 + near(lower))


def mulmod(left, right):
    top, low = split(right)
    return near(near(left * top) * 256.0 + left * low)


def dot(left, right):
    return jnp.dot(left, right, preferred_element_type=jnp.float32)


def dot_t(left, right):
    return lax.dot_general(
        left, right, (((1,), (1,)), ((), ())), preferred_element_type=jnp.float32
    )


def product_parts(left, right):
    order = left.shape[0]
    left_digits = digits(left)
    right_top, right_low = split(right)
    with_top = dot(left_digits, right_top.astype(jnp.bfloat16))
    with_low = dot(left_digits, right_low.astype(jnp.bfloat16))
    return with_top[:order], with_top[order:] + with_low[:order], with_low[order:]


def small_product(left, right):
    return fold_three(*product_parts(left, right))


def gram_tiles(tiles):
    order = tiles[0].shape[0]
    total = None
    for tile in tiles:
        both = digits(tile)
        term = dot_t(both, both)
        total = term if total is None else total + term
    return fold_three(
        total[:order, :order],
        total[:order, order:] + total[order:, :order],
        total[order:, order:],
    )


def power_inverse(number):
    result = None
    square = number
    for position in range(16):
        if 65519 >> position & 1:
            result = square if result is None else mulmod(result, square)
        if position < 15:
            square = mulmod(square, square)
    return result


def identity_of(order):
    rows = lax.broadcasted_iota(jnp.int32, (order, order), 0)
    lanes = lax.broadcasted_iota(jnp.int32, (order, order), 1)
    return jnp.where(rows == lanes, 1.0, 0.0).astype(jnp.float32)


class Elimination:
    def __init__(self, matrix):
        self.order = matrix.shape[0]
        self.done = 0
        self.work = jnp.concatenate([matrix, identity_of(self.order)], axis=1)

    def advance(self, columns):
        last = min(self.order, self.done + columns)
        for column in range(self.done, last):
            self.work = eliminated(self.work, column)
        self.done = last

    def result(self):
        self.advance(self.order)
        left = self.work[:, : self.order]
        diagonal = jnp.sum(left * identity_of(self.order), axis=1, keepdims=True)
        return mulmod(self.work[:, self.order :], power_inverse(diagonal))


def eliminated(work, column):
    order = work.shape[0]
    rows = lax.broadcasted_iota(jnp.int32, (order, 1), 0)
    entry = work[:, column : column + 1]
    usable = (entry != 0.0) & (rows >= column)
    first = jnp.min(jnp.where(usable, rows, order), axis=0, keepdims=True)
    chosen = rows == jnp.where(first == order, column, first)
    pivot_row = jnp.sum(jnp.where(chosen, work, 0.0), axis=0, keepdims=True)
    pivot = jnp.sum(jnp.where(chosen, entry, 0.0), axis=0, keepdims=True)
    swapped = jnp.where(chosen, work[column : column + 1, :], work)
    factor = jnp.where(chosen, entry[column : column + 1, :], entry)
    pivot_row = jnp.where(pivot == 0.0, 0.0, pivot_row)
    pivot = jnp.where(pivot == 0.0, 1.0, pivot)
    pivot_top, pivot_low = split(pivot)
    factor_top, factor_low = split(factor)
    upper = near(pivot_top * swapped - factor_top * pivot_row)
    reduced = near(upper * 256.0 + (pivot_low * swapped - factor_low * pivot_row))
    return jnp.where(rows == column, pivot_row, reduced)


def pack(values):
    rows = values.shape[0] // 4
    return jnp.concatenate([values[g * rows : (g + 1) * rows] for g in range(4)], axis=1)


def unpack(values):
    width = values.shape[1] // 4
    return jnp.concatenate([values[:, g * width : (g + 1) * width] for g in range(4)], axis=0)


def direct_squares(n_row, n_col):
    return n_row * n_col <= 64


def flipped(place, mask, count):
    assert count & (count - 1) == 0
    bit = 1
    moved = place
    while bit < count:
        if mask & bit:
            moved = moved + bit - 2 * bit * lax.rem(place // bit, 2)
        bit *= 2
    return moved


def kernel(
    n_row, n_col, cols_hbm,
    entries_hbm, now_hbm, prev_hbm, prev2_hbm,
    gram_hbm, square_hbm, inverse_hbm, inverse2_hbm, next_ref, later_ref,
    cols_ref, entries_ref, now_ref, older_ref, small_ref,
    tile16, tile_t, full_a, full_b, partial, spread, running, outgoing, incoming,
    gram_buf, square_row, square_col, square_all, order_ref, begin_ref,
    local_sem, send_sem, recv_sem, block_sem, partial_sem, fence_sem,
):
    my_row = lax.axis_index("row")
    my_col = lax.axis_index("col")
    tile_rows, slots, size = entries_ref.shape[:3]
    stored = tile_rows * slots
    order = now_ref.shape[0]
    share = now_ref.shape[1] // size
    half = n_row // 2
    rows = order // GROUPS
    direct = direct_squares(n_row, n_col)

    def row_peer(m):
        return flipped(my_row, m, n_row)

    def col_peer(m):
        return flipped(my_col, m, n_col)

    arrivals = [(now_hbm, now_ref, 0), (entries_hbm, entries_ref, 1)]
    arrivals += [(cols_hbm, cols_ref, 4), (prev_hbm, older_ref.at[0], 2), (prev2_hbm, older_ref.at[1], 2)]
    for i, source in enumerate([gram_hbm, square_hbm, inverse_hbm, inverse2_hbm]):
        arrivals.append((source, small_ref.at[i], 3))
    copies_in = [
        pltpu.make_async_copy(source, target, local_sem.at[i]) for source, target, i in arrivals
    ]

    def local_wait(ref, i):
        pltpu.make_async_copy(ref, ref, local_sem.at[i]).wait()

    pairs = [(m, k) for k in range(n_col) for m in range(n_row) if m or k]
    greeted = [(m, k) for m, k in pairs if m == 0 or k == 0]
    copies_in[0].start()
    barrier = pltpu.get_barrier_semaphore()
    for m, k in greeted:
        pl.semaphore_signal(
            barrier, inc=1, device_id=(row_peer(m), col_peer(k)), device_id_type=MESH
        )
    for copy in copies_in[1:]:
        copy.start()

    def remote(source, target, out, into, device):
        return pltpu.make_async_remote_copy(
            src_ref=source, dst_ref=target, send_sem=out, recv_sem=into,
            device_id=device, device_id_type=MESH,
        )

    def send(source, target, out, into, device):
        copy = remote(source, target, send_sem.at[out], into, device)
        copy.start()
        return copy

    def fence():
        pl.semaphore_signal(fence_sem, 1)
        pl.semaphore_wait(fence_sem, 1)

    def wait_in(ref, into):
        remote(ref, ref, send_sem.at[0], into, (my_row, my_col)).wait_recv()

    def wait_out(ref, out):
        remote(ref, ref, send_sem.at[out], recv_sem.at[0], (my_row, my_col)).wait_send()

    def tiles_of(values):
        return [values[:, t * size : (t + 1) * size] for t in range(share)]

    def load(ref):
        return tiles_of(near(ref[...].astype(jnp.float32)))

    def block(full, row):
        return full.at[pl.ds(row * share, share)]

    def joined(groups):
        return [jnp.concatenate([g[t] for g in groups], axis=0) for t in range(len(groups[0]))]

    def part(values, h):
        return values[h * rows : (h + 1) * rows]

    local_wait(now_ref, 0)
    current = load(now_ref)
    for h in range(GROUPS):
        for t in range(share):
            full_a[h][my_row * share + t] = part(current[t], h)
    pl.semaphore_wait(barrier, len(greeted))

    def gather_start(step, h, full):
        mine = block(full[h], my_row)
        for m in range(1, half):
            send(mine, mine, BLOCKS_OUT + step, block_sem.at[h, m], (row_peer(2 * m), my_col))
        send(mine, mine, BLOCKS_OUT + step, block_sem.at[h, 0], (row_peer(1), my_col))
        fence()

    def gather_pass(step, h, full, m):
        got = block(full[h], row_peer(2 * m))
        wait_in(got, block_sem.at[h, m])
        send(got, got, BLOCKS_OUT + step, block_sem.at[h, 0], (row_peer(1), my_col))
        fence()

    def gather_end(h, full):
        wait_in(full[h].at[pl.ds(0, half * share)], block_sem.at[h, 0])

    def third_of():
        middle = near(identity - small_product(inverse_old, gram_old))
        return -small_product(
            small_product(near(square_old + gram_old), middle), inverse_older
        )

    gather_start(0, 0, full_a)
    local_wait(entries_ref, 1)
    for i in range(stored):
        tile16[i] = entries_ref[i // slots, i % slots].astype(jnp.float32).astype(jnp.bfloat16)
    fence()
    for h in range(1, GROUPS):
        gather_start(0, h, full_a)
    local_wait(older_ref, 2)
    local_wait(small_ref, 3)
    earlier, earliest = load(older_ref.at[0]), load(older_ref.at[1])
    gram_old = near(small_ref[0].astype(jnp.float32))
    square_old = near(small_ref[1].astype(jnp.float32))
    inverse_old = near(small_ref[2].astype(jnp.float32))
    inverse_older = near(small_ref[3].astype(jnp.float32))
    identity = identity_of(order)
    local_wait(cols_ref, 4)
    cols = [cols_ref[i // slots, i % slots] for i in range(stored)]

    def as_int(flag):
        return jnp.where(flag, 1, 0).astype(jnp.int32)

    third = third_of()

    def rank_all():
        ranks = []
        for i in range(stored):
            rank = jnp.int32(0)
            for j in range(stored):
                if j != i:
                    rank = rank + as_int(cols[j] <= cols[i] if j < i else cols[j] < cols[i])
            ranks.append(rank)
        for k in range(stored):
            place = jnp.int32(0)
            for i in range(1, stored):
                place = place + jnp.where(ranks[i] == k, i, 0).astype(jnp.int32)
            order_ref[k] = place

    def count(tile, carry):
        below = jnp.int32(0)
        for i in range(stored):
            below = below + as_int(cols[i] < tile)
        begin_ref[tile] = below
        return carry

    for i in range(stored):
        turned = entries_ref[i // slots, i % slots].astype(jnp.float32).T
        at = i % slots * size
        tile_t[i // slots, at : at + size] = turned.astype(jnp.bfloat16)
    lax.fori_loop(0, n_row * share + 1, count, 0)
    for h in range(GROUPS):
        for m in range(1, half):
            gather_pass(0, h, full_a, m)
    rank_all()

    def forward(step, h, full):
        for r in range(tile_rows):
            picked = [digits(full[h][cols[r * slots + s]]) for s in range(slots)]
            total = dot(jnp.concatenate(picked, axis=1), tile_t[r])
            partial[step, h, my_col, r] = fold_two(total[:rows], total[rows:])
        own = partial.at[step, h, my_col]
        for m in range(1, n_col):
            send(own, own, PARTIAL_OUT + step, partial_sem.at[step, h], (my_row, col_peer(m)))
        fence()

    def partial_end(step, h):
        wait_in(partial.at[step, h, pl.ds(0, n_col - 1)], partial_sem.at[step, h])
        sums = []
        for r in range(tile_rows):
            total = partial[step, h, 0, r]
            for c in range(1, n_col):
                total = total + partial[step, h, c, r]
            sums.append(total)
        return sums

    for h in range(GROUPS):
        gather_end(h, full_a)
        forward(0, h, full_a)

    def summed(buffer, count):
        total = buffer[0]
        for r in range(1, count):
            total = total + buffer[r]
        return near(total)

    def to_row(buffer, out, into):
        own = buffer.at[my_row]
        for m in range(1, n_row):
            send(own, own, out, recv_sem.at[into], (row_peer(m), my_col))
        fence()

    def from_row(buffer, out, into):
        others = buffer.at[pl.ds(0, n_row - 1)]
        wait_in(others, recv_sem.at[into])
        wait_out(others, out)
        return summed(buffer, n_row)

    def square_start(step, applied):
        packed = pack(gram_tiles(joined(applied)))
        if direct:
            mine = my_row * n_col + my_col
            square_all[step, mine] = packed
            own = square_all.at[step, mine]
            for m, k in reversed(pairs):
                send(
                    own, own, SQUARE_ALL_OUT, recv_sem.at[SQUARE_ALL_IN + step],
                    (row_peer(m), col_peer(k)),
                )
            fence()
        else:
            square_row[my_row] = packed
            to_row(square_row, SQUARE_ROW_OUT, SQUARE_ROW_IN)

    def square_cols():
        if direct:
            return
        square_col[my_col] = from_row(square_row, SQUARE_ROW_OUT, SQUARE_ROW_IN)
        own = square_col.at[my_col]
        for m in range(1, n_col):
            send(own, own, SQUARE_COL_OUT, recv_sem.at[SQUARE_COL_IN], (my_row, col_peer(m)))
        fence()

    def square_end(step):
        if direct:
            others = square_all.at[step, pl.ds(0, n_row * n_col - 1)]
            wait_in(others, recv_sem.at[SQUARE_ALL_IN + step])
            wait_out(others, SQUARE_ALL_OUT)
            return unpack(summed(square_all.at[step], n_row * n_col))
        others = square_col.at[pl.ds(0, n_col - 1)]
        wait_in(others, recv_sem.at[SQUARE_COL_IN])
        wait_out(others, SQUARE_COL_OUT)
        return unpack(summed(square_col, n_col))

    def spread_out(step, h, projected):
        for r in range(tile_rows):
            both = digits(projected[r])
            for s in range(slots):
                spread[h, r * slots + s] = dot(both, tile16[r * slots + s])
        total = jnp.zeros((2 * rows, size), jnp.float32)
        running[h, 0] = total
        for i in range(stored):
            total = total + spread[h, order_ref[i]]
            running[h, i + 1] = total

        def finish_block(peer):
            for t in range(share):
                tile = peer * share + t
                sums = running[h, begin_ref[tile + 1]] - running[h, begin_ref[tile]]
                outgoing[step, h, tile] = fold_two(sums[:rows], sums[rows:])

        for m in range(half - 1, -1, -1):
            peer = row_peer(2 * m + 1)
            finish_block(peer)
            send(
                block(outgoing.at[step, h], peer), incoming.at[step, h, m],
                BLOCKS_OUT + step, block_sem.at[h, half + m], (row_peer(1), my_col),
            )
            fence()
        for m in range(half - 1, -1, -1):
            finish_block(row_peer(2 * m))

    def scatter_pass(step, h, m):
        wait_in(incoming.at[step, h, m], block_sem.at[h, half + m])
        peer = row_peer(2 * m)
        for t in range(share):
            outgoing[step, h, peer * share + t] = (
                outgoing[step, h, peer * share + t] + incoming[step, h, m, t]
            )
        send(
            block(outgoing.at[step, h], peer), incoming.at[step, h, half + m],
            BLOCKS_OUT + step, block_sem.at[h, half], (peer, my_col),
        )
        fence()

    def scatter_end(step, h):
        wait_in(incoming.at[step, h, pl.ds(0, half)], block_sem.at[h, half])
        applied = []
        for t in range(share):
            total = outgoing[step, h, my_row * share + t]
            for m in [0] + list(range(half + 1, n_row)):
                total = total + incoming[step, h, m, t]
            applied.append(near(total))
        return applied

    rest = None
    for step in range(2):
        projected = []
        if step:
            square_now = square_end(0)
            first = near(
                identity - small_product(near(square_now + gram_now), inverse_now)
            )
            rest = [fold_three(*product_parts(first, y)) for y in joined(before)]
        for h in range(GROUPS):
            sums = partial_end(step, h)
            if step:
                sums = [sums[r] + part(rest[r], h) for r in range(tile_rows)]
            projected.append([near(total) for total in sums])
            if h == GROUPS - 1:
                gram_buf[step, my_row] = pack(gram_tiles(joined(projected)))
                to_row(gram_buf.at[step], GRAM_OUT, GRAM_IN)
            spread_out(step, h, projected[h])
        before = projected
        if step:
            following = []
            for t in range(share):
                upper, mid, lower = product_parts(first, current[t])
                following.append(
                    whole(ready[t] + near(upper) * 15.0 + near(mid) * 256.0 + lower)
                )
                next_ref[:, t * size : (t + 1) * size] = following[t]
            earliest, earlier, current = earlier, current, [near(f) for f in following]
            inverse_older, inverse_old = inverse_old, inverse_now
            gram_old, square_old = gram_now, square_now
            third = third_of()
            fence()
        applied = []
        for turn in range(GROUPS + LAG):
            if turn < GROUPS:
                for m in range(half - 1, 0, -1):
                    scatter_pass(step, turn, m)
            if turn == GRAM_TURN:
                gram_now = unpack(from_row(gram_buf.at[step], GRAM_OUT, GRAM_IN))
                inverting = Elimination(gram_now)
                second = -small_product(gram_now, inverse_old)
                parts = []
                for t in range(share):
                    one = product_parts(second, earlier[t])
                    two = product_parts(third, earliest[t])
                    upper, mid, lower = [a + b for a, b in zip(one, two)]
                    parts.append(near(upper) * 15.0 + near(mid) * 256.0 + lower)
            if turn < LAG:
                continue
            h = turn - LAG
            if step and turn >= GROUPS - 1:
                inverting.advance(16 // LAG)
            applied.append(scatter_end(step, h))
            if step == 0:
                for t in range(share):
                    full_b[h][my_row * share + t] = near(applied[h][t] + part(parts[t], h))
                gather_start(1, h, full_b)
        ready = [near(a + b) for a, b in zip(joined(applied), parts)]
        square_start(step, applied)

        if step == 0:
            inverting.advance(4)
            for h in range(GROUPS):
                for m in range(1, half):
                    gather_pass(1, h, full_b, m)
                    inverting.advance(4)
            square_cols()
            for h in range(GROUPS):
                gather_end(h, full_b)
                forward(1, h, full_b)
            inverse_now = inverting.result()
            continue

        inverse_now = inverting.result()
        turned = [small_product(inverse_now, current[t]) for t in range(share)]
        fixed = []
        for t in range(share):
            upper, mid, lower = product_parts(gram_now, turned[t])
            done = near(upper) * 15.0 + near(mid) * 256.0 + lower
            fixed.append(near(ready[t] + current[t] - done))
        square_cols()
        square_now = square_end(1)
        for t in range(share):
            upper, mid, lower = product_parts(square_now, turned[t])
            done = near(upper) * 15.0 + near(mid) * 256.0 + lower
            later_ref[:, t * size : (t + 1) * size] = whole(fixed[t] - done)

    for step in range(2):
        wait_out(outgoing.at[:, :, pl.ds(0, (n_row - 1) * share)], BLOCKS_OUT + step)
        wait_out(partial.at[step, :, pl.ds(0, n_col - 1)], PARTIAL_OUT + step)


def body(
    n_row, n_col, entries, tile_cols, block_now, block_prev, block_prev2,
    gram_prev, square_prev, inverse_prev, inverse_prev2,
):
    tile_rows, slots, size = entries.shape[:3]
    order, width = block_now.shape
    share = width // size
    col_tiles = n_row * share
    stored = tile_rows * slots
    rows = order // GROUPS
    assert order % (8 * GROUPS) == 0
    assert tile_rows <= 4 and share <= 4 and n_row % 2 == 0

    f32 = jnp.float32
    vmem = pl.BlockSpec(memory_space=pltpu.VMEM)
    hbm = pl.BlockSpec(memory_space=pltpu.HBM)
    devices = n_row * n_col if direct_squares(n_row, n_col) else 1
    packed = (order // 4, order * 4)
    following, later = pl.pallas_call(
        functools.partial(kernel, n_row, n_col),
        out_shape=(pltpu.VMEM((order, width), f32),) * 2,
        in_specs=[hbm] * 9,
        out_specs=(vmem, vmem),
        scratch_shapes=[
            pltpu.SMEM(tile_cols.shape, jnp.int32),
            pltpu.VMEM(entries.shape, jnp.int32),
            pltpu.VMEM((order, width), jnp.int32),
            pltpu.VMEM((2, order, width), jnp.int32),
            pltpu.VMEM((4, order, order), jnp.int32),
            pltpu.VMEM((stored, size, size), jnp.bfloat16),
            pltpu.VMEM((tile_rows, slots * size, size), jnp.bfloat16),
            [pltpu.VMEM((col_tiles, rows, size), f32)] * GROUPS,
            [pltpu.VMEM((col_tiles, rows, size), f32)] * GROUPS,
            pltpu.VMEM((2, GROUPS, n_col, tile_rows, rows, size), f32),
            pltpu.VMEM((GROUPS, stored, 2 * rows, size), f32),
            pltpu.VMEM((GROUPS, stored + 1, 2 * rows, size), f32),
            pltpu.VMEM((2, GROUPS, col_tiles, rows, size), f32),
            pltpu.VMEM((2, GROUPS, n_row, share, rows, size), f32),
            pltpu.VMEM((2, n_row) + packed, f32),
            pltpu.VMEM((n_row,) + packed, f32),
            pltpu.VMEM((n_col,) + packed, f32),
            pltpu.VMEM((2, devices) + packed, f32),
            pltpu.SMEM((stored,), jnp.int32),
            pltpu.SMEM((col_tiles + 1,), jnp.int32),
            pltpu.SemaphoreType.DMA((5,)),
            pltpu.SemaphoreType.DMA((8,)),
            pltpu.SemaphoreType.DMA((5,)),
            pltpu.SemaphoreType.DMA((GROUPS, n_row)),
            pltpu.SemaphoreType.DMA((2, GROUPS)),
            pltpu.SemaphoreType.REGULAR,
        ],
        compiler_params=pltpu.CompilerParams(collective_id=0, has_side_effects=True),
    )(
        tile_cols, entries, block_now, block_prev, block_prev2,
        gram_prev, square_prev, inverse_prev, inverse_prev2,
    )
    return following / modulus, later / modulus


def solution(mesh):
    placed = (
        P("row", "col", None, None),
        P("row", "col"),
        P(None, ("col", "row")),
        P(None, ("col", "row")),
        P(None, ("col", "row")),
        P(),
        P(),
        P(),
        P(),
    )
    return jax.shard_map(
        functools.partial(body, mesh.shape["row"], mesh.shape["col"]),
        mesh=mesh,
        in_specs=placed,
        out_specs=(P(None, ("col", "row")), P(None, ("col", "row"))),
        check_vma=False,
    )
```

```python
import functools

import jax
import jax.numpy as jnp
from jax import lax
from jax.experimental import pallas as pl
from jax.experimental.pallas import tpu as pltpu
from jax.sharding import PartitionSpec as P

modulus = 65521.0
reciprocal = 1.0 / 65521.0
MESH = pl.DeviceIdType.MESH
GROUPS = 4
LAG = 4
GRAM_TURN = 2
BLOCKS_OUT, PARTIAL_OUT, GRAM_OUT, SQUARE_ROW_OUT, SQUARE_COL_OUT, SQUARE_ALL_OUT = 0, 2, 4, 5, 6, 7
GRAM_IN, SQUARE_ROW_IN, SQUARE_COL_IN, SQUARE_ALL_IN = 0, 1, 2, 3


def near(values):
    return values - jnp.floor(values * reciprocal + 0.5) * modulus


def whole(values):
    signed = near(values)
    return jnp.where(signed < 0.0, signed + modulus, signed)


def split(values):
    top = jnp.floor(values * (1.0 / 256.0) + 0.5)
    return top, values - top * 256.0


def digits(values):
    top, low = split(values)
    return jnp.concatenate([top, low], axis=0).astype(jnp.bfloat16)


def fold_two(top, low):
    return near(near(top) * 256.0 + low)


def fold_three(upper, middle, lower):
    return near(near(upper) * 15.0 + near(middle) * 256.0 + near(lower))


def mulmod(left, right):
    top, low = split(right)
    return near(near(left * top) * 256.0 + left * low)


def dot(left, right):
    return jnp.dot(left, right, preferred_element_type=jnp.float32)


def dot_t(left, right):
    return lax.dot_general(
        left, right, (((1,), (1,)), ((), ())), preferred_element_type=jnp.float32
    )


def product_parts(left, right):
    order = left.shape[0]
    left_digits = digits(left)
    right_top, right_low = split(right)
    with_top = dot(left_digits, right_top.astype(jnp.bfloat16))
    with_low = dot(left_digits, right_low.astype(jnp.bfloat16))
    return with_top[:order], with_top[order:] + with_low[:order], with_low[order:]


def small_product(left, right):
    return fold_three(*product_parts(left, right))


def gram_tiles(tiles):
    order = tiles[0].shape[0]
    total = None
    for tile in tiles:
        both = digits(tile)
        term = dot_t(both, both)
        total = term if total is None else total + term
    return fold_three(
        total[:order, :order],
        total[:order, order:] + total[order:, :order],
        total[order:, order:],
    )


def power_inverse(number):
    result = None
    square = number
    for position in range(16):
        if 65519 >> position & 1:
            result = square if result is None else mulmod(result, square)
        if position < 15:
            square = mulmod(square, square)
    return result


def identity_of(order):
    rows = lax.broadcasted_iota(jnp.int32, (order, order), 0)
    lanes = lax.broadcasted_iota(jnp.int32, (order, order), 1)
    return jnp.where(rows == lanes, 1.0, 0.0).astype(jnp.float32)


class Elimination:
    def __init__(self, matrix):
        self.order = matrix.shape[0]
        self.done = 0
        self.work = jnp.concatenate([matrix, identity_of(self.order)], axis=1)

    def advance(self, columns):
        last = min(self.order, self.done + columns)
        for column in range(self.done, last):
            self.work = eliminated(self.work, column)
        self.done = last

    def result(self):
        self.advance(self.order)
        left = self.work[:, : self.order]
        diagonal = jnp.sum(left * identity_of(self.order), axis=1, keepdims=True)
        return mulmod(self.work[:, self.order :], power_inverse(diagonal))


def eliminated(work, column):
    order = work.shape[0]
    rows = lax.broadcasted_iota(jnp.int32, (order, 1), 0)
    entry = work[:, column : column + 1]
    usable = (entry != 0.0) & (rows >= column)
    first = jnp.min(jnp.where(usable, rows, order), axis=0, keepdims=True)
    chosen = rows == jnp.where(first == order, column, first)
    pivot_row = jnp.sum(jnp.where(chosen, work, 0.0), axis=0, keepdims=True)
    pivot = jnp.sum(jnp.where(chosen, entry, 0.0), axis=0, keepdims=True)
    swapped = jnp.where(chosen, work[column : column + 1, :], work)
    factor = jnp.where(chosen, entry[column : column + 1, :], entry)
    pivot_row = jnp.where(pivot == 0.0, 0.0, pivot_row)
    pivot = jnp.where(pivot == 0.0, 1.0, pivot)
    pivot_top, pivot_low = split(pivot)
    factor_top, factor_low = split(factor)
    upper = near(pivot_top * swapped - factor_top * pivot_row)
    reduced = near(upper * 256.0 + (pivot_low * swapped - factor_low * pivot_row))
    return jnp.where(rows == column, pivot_row, reduced)


def pack(values):
    rows = values.shape[0] // 4
    return jnp.concatenate([values[g * rows : (g + 1) * rows] for g in range(4)], axis=1)


def unpack(values):
    width = values.shape[1] // 4
    return jnp.concatenate([values[:, g * width : (g + 1) * width] for g in range(4)], axis=0)


def direct_squares(n_row, n_col):
    return n_row * n_col <= 64


def flipped(place, mask, count):
    assert count & (count - 1) == 0
    bit = 1
    moved = place
    while bit < count:
        if mask & bit:
            moved = moved + bit - 2 * bit * lax.rem(place // bit, 2)
        bit *= 2
    return moved


def kernel(
    n_row, n_col, cols_hbm,
    entries_hbm, now_hbm, prev_hbm, prev2_hbm,
    gram_hbm, square_hbm, inverse_hbm, inverse2_hbm, next_ref, later_ref,
    cols_ref, entries_ref, now_ref, older_ref, small_ref,
    tile16, tile_t, full_a, full_b, partial, spread, running, outgoing, incoming,
    gram_buf, square_row, square_col, square_all, order_ref, begin_ref,
    local_sem, send_sem, recv_sem, block_sem, partial_sem, fence_sem,
):
    my_row = lax.axis_index("row")
    my_col = lax.axis_index("col")
    tile_rows, slots, size = entries_ref.shape[:3]
    stored = tile_rows * slots
    order = now_ref.shape[0]
    share = now_ref.shape[1] // size
    half = n_row // 2
    rows = order // GROUPS
    direct = direct_squares(n_row, n_col)

    def row_peer(m):
        return flipped(my_row, m, n_row)

    def col_peer(m):
        return flipped(my_col, m, n_col)

    arrivals = [(now_hbm, now_ref, 0), (entries_hbm, entries_ref, 1)]
    arrivals += [(cols_hbm, cols_ref, 4), (prev_hbm, older_ref.at[0], 2), (prev2_hbm, older_ref.at[1], 2)]
    for i, source in enumerate([gram_hbm, square_hbm, inverse_hbm, inverse2_hbm]):
        arrivals.append((source, small_ref.at[i], 3))
    copies_in = [
        pltpu.make_async_copy(source, target, local_sem.at[i]) for source, target, i in arrivals
    ]

    def local_wait(ref, i):
        pltpu.make_async_copy(ref, ref, local_sem.at[i]).wait()

    pairs = [(m, k) for k in range(n_col) for m in range(n_row) if m or k]
    greeted = [(m, k) for m, k in pairs if m == 0 or k == 0]
    copies_in[0].start()
    barrier = pltpu.get_barrier_semaphore()
    for m, k in sorted(greeted, key=lambda pair: -pair[0]):
        pl.semaphore_signal(
            barrier, inc=1, device_id=(row_peer(m), col_peer(k)), device_id_type=MESH
        )
    for copy in copies_in[1:]:
        copy.start()

    def remote(source, target, out, into, device):
        return pltpu.make_async_remote_copy(
            src_ref=source, dst_ref=target, send_sem=out, recv_sem=into,
            device_id=device, device_id_type=MESH,
        )

    def send(source, target, out, into, device):
        copy = remote(source, target, send_sem.at[out], into, device)
        copy.start()
        return copy

    def fence():
        pl.semaphore_signal(fence_sem, 1)
        pl.semaphore_wait(fence_sem, 1)

    def wait_in(ref, into):
        remote(ref, ref, send_sem.at[0], into, (my_row, my_col)).wait_recv()

    def wait_out(ref, out):
        remote(ref, ref, send_sem.at[out], recv_sem.at[0], (my_row, my_col)).wait_send()

    def tiles_of(values):
        return [values[:, t * size : (t + 1) * size] for t in range(share)]

    def load(ref):
        return tiles_of(near(ref[...].astype(jnp.float32)))

    def block(full, row):
        return full.at[pl.ds(row * share, share)]

    def joined(groups):
        return [jnp.concatenate([g[t] for g in groups], axis=0) for t in range(len(groups[0]))]

    def part(values, h):
        return values[h * rows : (h + 1) * rows]

    local_wait(now_ref, 0)
    current = load(now_ref)
    for h in range(GROUPS):
        for t in range(share):
            full_a[h][my_row * share + t] = part(current[t], h)
    pl.semaphore_wait(barrier, len(greeted))

    def gather_start(step, h, full):
        mine = block(full[h], my_row)
        for m in range(1, half):
            send(mine, mine, BLOCKS_OUT + step, block_sem.at[h, m], (row_peer(2 * m), my_col))
        send(mine, mine, BLOCKS_OUT + step, block_sem.at[h, 0], (row_peer(1), my_col))
        fence()

    def gather_pass(step, h, full, m):
        got = block(full[h], row_peer(2 * m))
        wait_in(got, block_sem.at[h, m])
        send(got, got, BLOCKS_OUT + step, block_sem.at[h, 0], (row_peer(1), my_col))
        fence()

    def gather_end(h, full):
        wait_in(full[h].at[pl.ds(0, half * share)], block_sem.at[h, 0])

    def third_of():
        middle = near(identity - small_product(inverse_old, gram_old))
        return -small_product(
            small_product(near(square_old + gram_old), middle), inverse_older
        )

    gather_start(0, 0, full_a)
    local_wait(entries_ref, 1)
    for i in range(stored):
        tile16[i] = entries_ref[i // slots, i % slots].astype(jnp.float32).astype(jnp.bfloat16)
    fence()
    for h in range(1, GROUPS):
        gather_start(0, h, full_a)
    local_wait(older_ref, 2)
    local_wait(small_ref, 3)
    earlier, earliest = load(older_ref.at[0]), load(older_ref.at[1])
    gram_old = near(small_ref[0].astype(jnp.float32))
    square_old = near(small_ref[1].astype(jnp.float32))
    inverse_old = near(small_ref[2].astype(jnp.float32))
    inverse_older = near(small_ref[3].astype(jnp.float32))
    identity = identity_of(order)
    local_wait(cols_ref, 4)
    cols = [cols_ref[i // slots, i % slots] for i in range(stored)]

    def as_int(flag):
        return jnp.where(flag, 1, 0).astype(jnp.int32)

    third = third_of()

    def rank_all():
        ranks = []
        for i in range(stored):
            rank = jnp.int32(0)
            for j in range(stored):
                if j != i:
                    rank = rank + as_int(cols[j] <= cols[i] if j < i else cols[j] < cols[i])
            ranks.append(rank)
        for k in range(stored):
            place = jnp.int32(0)
            for i in range(1, stored):
                place = place + jnp.where(ranks[i] == k, i, 0).astype(jnp.int32)
            order_ref[k] = place

    def count(tile, carry):
        below = jnp.int32(0)
        for i in range(stored):
            below = below + as_int(cols[i] < tile)
        begin_ref[tile] = below
        return carry

    for i in range(stored):
        turned = entries_ref[i // slots, i % slots].astype(jnp.float32).T
        at = i % slots * size
        tile_t[i // slots, at : at + size] = turned.astype(jnp.bfloat16)
    lax.fori_loop(0, n_row * share + 1, count, 0)
    for h in range(GROUPS):
        for m in range(1, half):
            gather_pass(0, h, full_a, m)
    rank_all()

    def forward(step, h, full):
        for r in range(tile_rows):
            picked = [digits(full[h][cols[r * slots + s]]) for s in range(slots)]
            total = dot(jnp.concatenate(picked, axis=1), tile_t[r])
            partial[step, h, my_col, r] = fold_two(total[:rows], total[rows:])
        own = partial.at[step, h, my_col]
        for m in range(1, n_col):
            send(own, own, PARTIAL_OUT + step, partial_sem.at[step, h], (my_row, col_peer(m)))
        fence()

    def partial_end(step, h):
        wait_in(partial.at[step, h, pl.ds(0, n_col - 1)], partial_sem.at[step, h])
        sums = []
        for r in range(tile_rows):
            total = partial[step, h, 0, r]
            for c in range(1, n_col):
                total = total + partial[step, h, c, r]
            sums.append(total)
        return sums

    for h in range(GROUPS):
        gather_end(h, full_a)
        forward(0, h, full_a)

    def summed(buffer, count):
        total = buffer[0]
        for r in range(1, count):
            total = total + buffer[r]
        return near(total)

    def to_row(buffer, out, into):
        own = buffer.at[my_row]
        for m in range(1, n_row):
            send(own, own, out, recv_sem.at[into], (row_peer(m), my_col))
        fence()

    def from_row(buffer, out, into):
        others = buffer.at[pl.ds(0, n_row - 1)]
        wait_in(others, recv_sem.at[into])
        wait_out(others, out)
        return summed(buffer, n_row)

    def square_start(step, applied):
        packed = pack(gram_tiles(joined(applied)))
        if direct:
            mine = my_row * n_col + my_col
            square_all[step, mine] = packed
            own = square_all.at[step, mine]
            for m, k in reversed(pairs):
                send(
                    own, own, SQUARE_ALL_OUT, recv_sem.at[SQUARE_ALL_IN + step],
                    (row_peer(m), col_peer(k)),
                )
            fence()
        else:
            square_row[my_row] = packed
            to_row(square_row, SQUARE_ROW_OUT, SQUARE_ROW_IN)

    def square_cols():
        if direct:
            return
        square_col[my_col] = from_row(square_row, SQUARE_ROW_OUT, SQUARE_ROW_IN)
        own = square_col.at[my_col]
        for m in range(1, n_col):
            send(own, own, SQUARE_COL_OUT, recv_sem.at[SQUARE_COL_IN], (my_row, col_peer(m)))
        fence()

    def square_end(step):
        if direct:
            others = square_all.at[step, pl.ds(0, n_row * n_col - 1)]
            wait_in(others, recv_sem.at[SQUARE_ALL_IN + step])
            wait_out(others, SQUARE_ALL_OUT)
            return unpack(summed(square_all.at[step], n_row * n_col))
        others = square_col.at[pl.ds(0, n_col - 1)]
        wait_in(others, recv_sem.at[SQUARE_COL_IN])
        wait_out(others, SQUARE_COL_OUT)
        return unpack(summed(square_col, n_col))

    def spread_out(step, h, projected):
        for r in range(tile_rows):
            both = digits(projected[r])
            for s in range(slots):
                spread[h, r * slots + s] = dot(both, tile16[r * slots + s])
        total = jnp.zeros((2 * rows, size), jnp.float32)
        running[h, 0] = total
        for i in range(stored):
            total = total + spread[h, order_ref[i]]
            running[h, i + 1] = total

        def finish_block(peer):
            for t in range(share):
                tile = peer * share + t
                sums = running[h, begin_ref[tile + 1]] - running[h, begin_ref[tile]]
                outgoing[step, h, tile] = fold_two(sums[:rows], sums[rows:])

        for m in range(half - 1, -1, -1):
            peer = row_peer(2 * m + 1)
            finish_block(peer)
            send(
                block(outgoing.at[step, h], peer), incoming.at[step, h, m],
                BLOCKS_OUT + step, block_sem.at[h, half + m], (row_peer(1), my_col),
            )
            fence()
        for m in range(half - 1, -1, -1):
            finish_block(row_peer(2 * m))

    def scatter_pass(step, h, m):
        wait_in(incoming.at[step, h, m], block_sem.at[h, half + m])
        peer = row_peer(2 * m)
        for t in range(share):
            outgoing[step, h, peer * share + t] = (
                outgoing[step, h, peer * share + t] + incoming[step, h, m, t]
            )
        send(
            block(outgoing.at[step, h], peer), incoming.at[step, h, half + m],
            BLOCKS_OUT + step, block_sem.at[h, half], (peer, my_col),
        )
        fence()

    def scatter_end(step, h):
        wait_in(incoming.at[step, h, pl.ds(0, half)], block_sem.at[h, half])
        applied = []
        for t in range(share):
            total = outgoing[step, h, my_row * share + t]
            for m in [0] + list(range(half + 1, n_row)):
                total = total + incoming[step, h, m, t]
            applied.append(near(total))
        return applied

    rest = None
    for step in range(2):
        projected = []
        if step:
            square_now = square_end(0)
            first = near(
                identity - small_product(near(square_now + gram_now), inverse_now)
            )
            rest = [fold_three(*product_parts(first, y)) for y in joined(before)]
        for h in range(GROUPS):
            sums = partial_end(step, h)
            if step:
                sums = [sums[r] + part(rest[r], h) for r in range(tile_rows)]
            projected.append([near(total) for total in sums])
            if h == GROUPS - 1:
                gram_buf[step, my_row] = pack(gram_tiles(joined(projected)))
                to_row(gram_buf.at[step], GRAM_OUT, GRAM_IN)
            spread_out(step, h, projected[h])
        before = projected
        if step:
            following = []
            for t in range(share):
                upper, mid, lower = product_parts(first, current[t])
                following.append(
                    whole(ready[t] + near(upper) * 15.0 + near(mid) * 256.0 + lower)
                )
                next_ref[:, t * size : (t + 1) * size] = following[t]
            earliest, earlier, current = earlier, current, [near(f) for f in following]
            inverse_older, inverse_old = inverse_old, inverse_now
            gram_old, square_old = gram_now, square_now
            third = third_of()
            fence()
        applied = []
        for turn in range(GROUPS + LAG):
            if turn < GROUPS:
                for m in range(half - 1, 0, -1):
                    scatter_pass(step, turn, m)
            if turn == GRAM_TURN:
                gram_now = unpack(from_row(gram_buf.at[step], GRAM_OUT, GRAM_IN))
                inverting = Elimination(gram_now)
                second = -small_product(gram_now, inverse_old)
                parts = []
                for t in range(share):
                    one = product_parts(second, earlier[t])
                    two = product_parts(third, earliest[t])
                    upper, mid, lower = [a + b for a, b in zip(one, two)]
                    parts.append(near(upper) * 15.0 + near(mid) * 256.0 + lower)
            if turn < LAG:
                continue
            h = turn - LAG
            if step and turn >= GROUPS - 1:
                inverting.advance(16 // LAG)
            applied.append(scatter_end(step, h))
            if step == 0:
                for t in range(share):
                    full_b[h][my_row * share + t] = near(applied[h][t] + part(parts[t], h))
                gather_start(1, h, full_b)
        ready = [near(a + b) for a, b in zip(joined(applied), parts)]
        square_start(step, applied)

        if step == 0:
            inverting.advance(4)
            for h in range(GROUPS):
                for m in range(1, half):
                    gather_pass(1, h, full_b, m)
                    inverting.advance(4)
            square_cols()
            for h in range(GROUPS):
                gather_end(h, full_b)
                forward(1, h, full_b)
            inverse_now = inverting.result()
            continue

        inverse_now = inverting.result()
        turned = [small_product(inverse_now, current[t]) for t in range(share)]
        fixed = []
        for t in range(share):
            upper, mid, lower = product_parts(gram_now, turned[t])
            done = near(upper) * 15.0 + near(mid) * 256.0 + lower
            fixed.append(near(ready[t] + current[t] - done))
        square_cols()
        square_now = square_end(1)
        for t in range(share):
            upper, mid, lower = product_parts(square_now, turned[t])
            done = near(upper) * 15.0 + near(mid) * 256.0 + lower
            later_ref[:, t * size : (t + 1) * size] = whole(fixed[t] - done)

    for step in range(2):
        wait_out(outgoing.at[:, :, pl.ds(0, (n_row - 1) * share)], BLOCKS_OUT + step)
        wait_out(partial.at[step, :, pl.ds(0, n_col - 1)], PARTIAL_OUT + step)


def body(
    n_row, n_col, entries, tile_cols, block_now, block_prev, block_prev2,
    gram_prev, square_prev, inverse_prev, inverse_prev2,
):
    tile_rows, slots, size = entries.shape[:3]
    order, width = block_now.shape
    share = width // size
    col_tiles = n_row * share
    stored = tile_rows * slots
    rows = order // GROUPS
    assert order % (8 * GROUPS) == 0
    assert tile_rows <= 4 and share <= 4 and n_row % 2 == 0

    f32 = jnp.float32
    vmem = pl.BlockSpec(memory_space=pltpu.VMEM)
    hbm = pl.BlockSpec(memory_space=pltpu.HBM)
    devices = n_row * n_col if direct_squares(n_row, n_col) else 1
    packed = (order // 4, order * 4)
    following, later = pl.pallas_call(
        functools.partial(kernel, n_row, n_col),
        out_shape=(pltpu.VMEM((order, width), f32),) * 2,
        in_specs=[hbm] * 9,
        out_specs=(vmem, vmem),
        scratch_shapes=[
            pltpu.SMEM(tile_cols.shape, jnp.int32),
            pltpu.VMEM(entries.shape, jnp.int32),
            pltpu.VMEM((order, width), jnp.int32),
            pltpu.VMEM((2, order, width), jnp.int32),
            pltpu.VMEM((4, order, order), jnp.int32),
            pltpu.VMEM((stored, size, size), jnp.bfloat16),
            pltpu.VMEM((tile_rows, slots * size, size), jnp.bfloat16),
            [pltpu.VMEM((col_tiles, rows, size), f32)] * GROUPS,
            [pltpu.VMEM((col_tiles, rows, size), f32)] * GROUPS,
            pltpu.VMEM((2, GROUPS, n_col, tile_rows, rows, size), f32),
            pltpu.VMEM((GROUPS, stored, 2 * rows, size), f32),
            pltpu.VMEM((GROUPS, stored + 1, 2 * rows, size), f32),
            pltpu.VMEM((2, GROUPS, col_tiles, rows, size), f32),
            pltpu.VMEM((2, GROUPS, n_row, share, rows, size), f32),
            pltpu.VMEM((2, n_row) + packed, f32),
            pltpu.VMEM((n_row,) + packed, f32),
            pltpu.VMEM((n_col,) + packed, f32),
            pltpu.VMEM((2, devices) + packed, f32),
            pltpu.SMEM((stored,), jnp.int32),
            pltpu.SMEM((col_tiles + 1,), jnp.int32),
            pltpu.SemaphoreType.DMA((5,)),
            pltpu.SemaphoreType.DMA((8,)),
            pltpu.SemaphoreType.DMA((5,)),
            pltpu.SemaphoreType.DMA((GROUPS, n_row)),
            pltpu.SemaphoreType.DMA((2, GROUPS)),
            pltpu.SemaphoreType.REGULAR,
        ],
        compiler_params=pltpu.CompilerParams(collective_id=0, has_side_effects=True),
    )(
        tile_cols, entries, block_now, block_prev, block_prev2,
        gram_prev, square_prev, inverse_prev, inverse_prev2,
    )
    return following / modulus, later / modulus


def solution(mesh):
    placed = (
        P("row", "col", None, None),
        P("row", "col"),
        P(None, ("col", "row")),
        P(None, ("col", "row")),
        P(None, ("col", "row")),
        P(),
        P(),
        P(),
        P(),
    )
    return jax.shard_map(
        functools.partial(body, mesh.shape["row"], mesh.shape["col"]),
        mesh=mesh,
        in_specs=placed,
        out_specs=(P(None, ("col", "row")), P(None, ("col", "row"))),
        check_vma=False,
    )
```
